32 devices in a mesh: dp: 8 (over y, x, core), seq: 4 (over z).
Axes of the slice: x: 2, y: 2, z: 4, core: 2. Of those that a mesh axis runs over, the one named last changes fastest.
Arguments:
- values: bfloat16 [8, 1024, 512], P('dp', 'seq'), may hold values from -6 to 6
- gates_first: bfloat16 [8, 1024, 512], P('dp', 'seq'), may hold values from -6 to 6
- gates_second: bfloat16 [8, 1024, 512], P('dp', 'seq'), may hold values from -6 to 6
- filter_early: float32 [1024, 512], P('seq'), may hold values from -4 to 4
- filter_late: float32 [1024, 512], P('seq'), may hold values from -4 to 4
- skip_early: float32 [1024], P('seq'), may hold values from 0.1 to 1.9
- skip_late: float32 [1024], P('seq'), may hold values from 0.1 to 1.9
- targets: bfloat16 [8, 512, 1024], P('dp', 'seq'), may hold values from -6 to 6
- negative_rows: int32 [8, 8, 100], P('dp', 'seq'), may hold values from 0 to 1023
- recording_ids: int32 [8], replicated, may hold values from 0 to 3
Outputs:
- values_grad: bfloat16 [8, 1024, 512], P('dp', 'seq')
- first_grad: bfloat16 [8, 1024, 512], P('dp', 'seq')
- second_grad: bfloat16 [8, 1024, 512], P('dp', 'seq')
- early_grad: float32 [1024, 512], P('seq')
- late_grad: float32 [1024, 512], P('seq')
The draws below stay inside these ranges and needn't reach their ends.
All inputs are finite; a program needn't handle non-finite values.
Results may differ from the reference program's by a relative error of at most 0.014.
Values may be sent and summed in bfloat16 or wider, within the bound.
A program may use at most 128 MiB of HBM per device.

```python
import math
import jax
import jax.numpy as jnp
from jax import lax

D = 1024
SEGMENT = 128
BLOCK = 64
NEGS = 100
FRAMES = 512
RECS = 8
N_SEQ = 4


def filter_draw(base_key):
    rate_key, noise_key = jax.random.split(base_key)
    decay_rate = jnp.exp(jax.random.uniform(rate_key, (D, 1), jnp.float32, math.log(0.5 / FRAMES), math.log(1.0 / 40.0)))
    positions = jnp.arange(FRAMES, dtype=jnp.float32)[None, :]
    envelope = jnp.exp(-decay_rate * positions)
    energy = (1.0 - jnp.exp(-2.0 * decay_rate * FRAMES)) / (1.0 - jnp.exp(-2.0 * decay_rate))
    jitter = jnp.clip(jax.random.normal(noise_key, (D, FRAMES), jnp.float32), -3.5, 3.5)
    return jitter * envelope / jnp.sqrt(energy)


def draw_filter_early(key, part):
    return filter_draw(jax.random.fold_in(key, 11))


def draw_filter_late(key, part):
    return filter_draw(jax.random.fold_in(key, 23))


def with_ends(entries, key, least, largest):
    place = [jax.random.randint(jax.random.fold_in(key, axis), (), 0, length) for axis, length in enumerate(entries.shape)]
    widest = entries.shape.index(max(entries.shape))
    neighbour = place[:widest] + [(place[widest] + 1) % entries.shape[widest]] + place[widest + 1:]
    return entries.at[tuple(place)].set(least).at[tuple(neighbour)].set(largest)


def steps_of(stream_key, dims, cuts, least, largest):
    def one(position, parts):
        steps = jax.random.uniform(jax.random.fold_in(jax.random.fold_in(stream_key, 6), position), (parts,), jnp.float32, least / len(cuts), largest / len(cuts))
        return jnp.repeat(jnp.exp(steps), dims[position] // parts).reshape((-1,) + (1,) * (len(dims) - position - 1))

    gain = one(*cuts[0])
    for cut in cuts[1:]:
        gain = gain * one(*cut)
    return gain


def centred(stream_key, dims, width, limit, cuts=(), kind=jnp.bfloat16):
    drawn = width * jax.random.normal(stream_key, dims, jnp.float32)
    if cuts:
        drawn = drawn * steps_of(stream_key, dims, cuts, -0.22, 0.18)
    return jnp.clip(drawn, -limit, limit).astype(kind)


def setup_inputs(seed: int = 0) -> dict:
    seeds = jax.random.split(jax.random.key(seed), 11)
    values = centred(seeds[0], (RECS, D, FRAMES), 1.0, 6.0, ((0, 8), (1, 4)))
    gates_first = centred(seeds[1], (RECS, D, FRAMES), 1.0, 6.0, ((0, 8), (1, 4)))
    gates_second = centred(seeds[2], (RECS, D, FRAMES), 1.0, 6.0, ((0, 8), (1, 4)))
    filter_early = draw_filter_early(jax.random.fold_in(seeds[10], 71), 0)
    filter_late = draw_filter_late(jax.random.fold_in(seeds[10], 71), 0)
    skip_early = jnp.clip(1.0 + 0.18 * jax.random.normal(seeds[5], (D,), jnp.float32), 0.1, 1.9)
    skip_late = jnp.clip(1.0 + 0.18 * jax.random.normal(seeds[6], (D,), jnp.float32), 0.1, 1.9)
    targets = centred(seeds[7], (RECS, FRAMES, D), 1.0, 6.0, ((0, 8), (1, 4)))
    negative_rows = with_ends(jax.random.randint(seeds[8], (RECS, FRAMES // BLOCK, NEGS), 0, RECS * SEGMENT), jax.random.fold_in(seeds[8], 1), 0, (RECS * SEGMENT) - 1).astype(jnp.int32)
    recording_ids = with_ends(jax.random.randint(seeds[9], (RECS,), 0, RECS // 2), jax.random.fold_in(seeds[9], 1), 0, (RECS // 2) - 1).astype(jnp.int32)
    return dict(values=values, gates_first=gates_first, gates_second=gates_second, filter_early=filter_early, filter_late=filter_late, skip_early=skip_early, skip_late=skip_late, targets=targets, negative_rows=negative_rows, recording_ids=recording_ids)


EPSILON = 1e-06
INVERSE_TEMP = 10.0
LOSS_SCALE = 256.0

def causal_conv(kernel, signal):
    length = signal.shape[-1]
    spectra = jnp.fft.rfft(signal, n=2 * length) * jnp.fft.rfft(kernel, n=2 * length)
    return jnp.fft.irfft(spectra, n=2 * length)[..., :length]

def causal_adjoint(kernel, cotangent):
    length = cotangent.shape[-1]
    spectra = jnp.fft.rfft(cotangent, n=2 * length) * jnp.conj(jnp.fft.rfft(kernel, n=2 * length))
    return jnp.fft.irfft(spectra, n=2 * length)[..., :length]

def reference(values, gates_first, gates_second, filter_early, filter_late, skip_early, skip_late, targets, negative_rows, recording_ids):

    def forward(stream):
        signal = stream[0].astype(jnp.float32)
        inner_gate = stream[1].astype(jnp.float32)
        outer_gate = stream[2].astype(jnp.float32)
        mixed_one = causal_conv(filter_early, signal) + skip_early[:, None] * signal
        hidden = inner_gate * mixed_one
        mixed_two = causal_conv(filter_late, hidden) + skip_late[:, None] * hidden
        return (mixed_one, hidden, mixed_two, outer_gate * mixed_two)
    output = lax.map(lambda stream: forward(stream)[3], (values, gates_first, gates_second))
    output_rows = jnp.transpose(output, (0, 2, 1))
    radius = jnp.sqrt(lax.optimization_barrier(jnp.sum(output_rows * output_rows, axis=-1, keepdims=True)) + EPSILON)
    unit_rows = output_rows / radius
    anchors = unit_rows.astype(jnp.bfloat16)
    target_full = targets.astype(jnp.float32)
    unit_target = (target_full / jnp.sqrt(lax.optimization_barrier(jnp.sum(target_full * target_full, axis=-1, keepdims=True)) + EPSILON)).astype(jnp.bfloat16)
    block_count = SEGMENT // BLOCK
    anchor_split = anchors.reshape(RECS, N_SEQ, SEGMENT, D).transpose(1, 0, 2, 3)
    target_split = unit_target.reshape(RECS, N_SEQ, SEGMENT, D).transpose(1, 0, 2, 3)
    index_split = negative_rows.reshape(RECS, N_SEQ, block_count, NEGS).transpose(1, 0, 2, 3)
    positions = jnp.arange(RECS * SEGMENT, dtype=jnp.int32)
    pool_ids = recording_ids[positions // SEGMENT]

    def segment_grad(inputs):
        anchor_seg, target_seg, index_seg = inputs
        pool_rows = target_seg.reshape(RECS * SEGMENT, D)

        def record_grad(members):
            anchor_rows, target_rows, index_rows, label = members
            counts = lax.optimization_barrier(jnp.sum((index_rows[:, :, None] == positions[None, None, :]).astype(jnp.float32), axis=1))
            counts = counts * (pool_ids != label).astype(jnp.float32)[None, :]
            counts = jnp.repeat(counts, BLOCK, axis=0)
            scores = jnp.dot(anchor_rows, pool_rows.T, preferred_element_type=jnp.float32) * INVERSE_TEMP
            weights = counts * jnp.exp(scores)
            target_self = target_rows.astype(jnp.float32)
            positive = jnp.exp(lax.optimization_barrier(jnp.sum(anchor_rows.astype(jnp.float32) * target_self, axis=-1)) * INVERSE_TEMP)
            totals = positive + lax.optimization_barrier(jnp.sum(weights, axis=-1))
            numerator = jnp.dot(weights.astype(jnp.bfloat16), pool_rows, preferred_element_type=jnp.float32)
            return ((positive / totals - 1.0)[:, None] * target_self + numerator / totals[:, None]) * (INVERSE_TEMP * LOSS_SCALE)
        return lax.map(record_grad, (anchor_seg, target_seg, index_seg, recording_ids))
    anchor_grad = lax.map(segment_grad, (anchor_split, target_split, index_split))
    anchor_grad = anchor_grad.transpose(1, 0, 2, 3).reshape(RECS, FRAMES, D)
    frame_grad = (anchor_grad - unit_rows * lax.optimization_barrier(jnp.sum(unit_rows * anchor_grad, axis=-1, keepdims=True))) / radius
    output_grad = jnp.transpose(frame_grad, (0, 2, 1))

    def backward(stream):
        mixed_one, hidden, mixed_two, unused = forward((stream[0], stream[1], stream[2]))
        signal = stream[0].astype(jnp.float32)
        inner_gate = stream[1].astype(jnp.float32)
        outer_gate = stream[2].astype(jnp.float32)
        cotangent = stream[3]
        second_part = (cotangent * mixed_two).astype(jnp.bfloat16)
        late_drive = cotangent * outer_gate
        hidden_grad = causal_adjoint(filter_late, late_drive) + skip_late[:, None] * late_drive
        late_update = causal_adjoint(hidden, late_drive)
        first_part = (hidden_grad * mixed_one).astype(jnp.bfloat16)
        early_drive = hidden_grad * inner_gate
        values_part = (causal_adjoint(filter_early, early_drive) + skip_early[:, None] * early_drive).astype(jnp.bfloat16)
        early_update = causal_adjoint(signal, early_drive)
        return (values_part, first_part, second_part, early_update, late_update)
    results = lax.map(backward, (values, gates_first, gates_second, output_grad))
    early_grad = lax.optimization_barrier(jnp.sum(results[3], axis=0)) / FRAMES
    late_grad = lax.optimization_barrier(jnp.sum(results[4], axis=0)) / FRAMES
    return (results[0], results[1], results[2], early_grad, late_grad)
```

```python
import functools
import math

import jax
import jax.numpy as jnp
import numpy as np
from jax import lax
from jax.experimental import pallas as pl
from jax.experimental.pallas import tpu as pltpu
from jax.sharding import PartitionSpec as P

EPSILON = 1e-06
INVERSE_TEMP = 10.0
LOSS_SCALE = 256.0
MESH = pl.DeviceIdType.MESH
F32 = jnp.float32
BF16 = jnp.bfloat16
TABLE_BYTES = 16 * 1024 * 1024
INNER_WIDTH = 128
GRID_CHIPS = 4
VMEM_BYTES = 40 * 1024 * 1024
HIGHEST = lax.Precision.HIGHEST


def shortened(value):

    def short(part):
        return part.astype(jnp.bfloat16) if part.dtype == jnp.float32 else part

    return jax.tree.map(short, value)


def twiddle(row_count, column_count, length, direction):
    product = (
        jnp.arange(row_count, dtype=jnp.int32)[:, None]
        * jnp.arange(column_count, dtype=jnp.int32)[None, :]
        % length
    )
    angles = direction * 2.0 * math.pi / length * product.astype(jnp.float32)
    return (jnp.cos(angles), jnp.sin(angles))


def complex_table(cosines, sines, with_imaginary):
    upper = jnp.concatenate([cosines, sines], axis=1)
    if not with_imaginary:
        return upper
    lower = jnp.concatenate([-sines, cosines], axis=1)
    return jnp.concatenate([upper, lower], axis=0)


def transform(real_part, imaginary, direction, length):
    used = real_part.shape[-1]
    with_imaginary = imaginary is not None
    outer_size = length // INNER_WIDTH
    used_rows = used // INNER_WIDTH
    lead = real_part.shape[:-1]
    folded_real = real_part.reshape(lead + (used_rows, INNER_WIDTH))
    cosines, sines = twiddle(used_rows, outer_size, outer_size, direction)
    table = complex_table(cosines, sines, with_imaginary)
    if with_imaginary:
        stacked = jnp.concatenate(
            [folded_real, imaginary.reshape(lead + (used_rows, INNER_WIDTH))], axis=-2
        )
    else:
        stacked = folded_real
    section = jnp.einsum("...ab,ak->...kb", stacked, table, precision=HIGHEST)
    section_real = section[..., :outer_size, :]
    section_imaginary = section[..., outer_size:, :]
    turn_cosine, turn_sine = twiddle(outer_size, INNER_WIDTH, length, direction)
    turned_real = section_real * turn_cosine - section_imaginary * turn_sine
    turned_imaginary = section_real * turn_sine + section_imaginary * turn_cosine
    inner_cosine, inner_sine = twiddle(INNER_WIDTH, INNER_WIDTH, INNER_WIDTH, direction)
    inner_table = complex_table(inner_cosine, inner_sine, True)
    second = jnp.einsum(
        "...ab,bk->...ak",
        jnp.concatenate([turned_real, turned_imaginary], axis=-1),
        inner_table,
        precision=HIGHEST,
    )
    final_real = jnp.swapaxes(second[..., :INNER_WIDTH], -1, -2).reshape(lead + (length,))
    final_imaginary = jnp.swapaxes(second[..., INNER_WIDTH:], -1, -2).reshape(lead + (length,))
    return (final_real, final_imaginary)


def spectrum(signal):
    return transform(signal, None, -1.0, 2 * signal.shape[-1])


def split_pair(first_signal, second_signal):
    spec_real, spec_imaginary = transform(
        first_signal, second_signal, -1.0, 2 * first_signal.shape[-1]
    )
    mirror_real = jnp.roll(jnp.flip(spec_real, -1), 1, -1)
    mirror_imaginary = jnp.roll(jnp.flip(spec_imaginary, -1), 1, -1)
    first_spec = ((spec_real + mirror_real) * 0.5, (spec_imaginary - mirror_imaginary) * 0.5)
    second_spec = ((spec_imaginary + mirror_imaginary) * 0.5, (mirror_real - spec_real) * 0.5)
    return (first_spec, second_spec)


def multiply(left_side, right_side):
    return (
        left_side[0] * right_side[0] - left_side[1] * right_side[1],
        left_side[0] * right_side[1] + left_side[1] * right_side[0],
    )


def conjugate(spec):
    return (spec[0], -spec[1])


def combine(left_side, right_side):
    return (left_side[0] - right_side[1], left_side[1] + right_side[0])


def inverse(spec, frames):
    length = spec[0].shape[-1]
    out_real, out_imaginary = transform(spec[0], spec[1], 1.0, length)
    factor = 1.0 / length
    return (out_real[..., :frames] * factor, out_imaginary[..., :frames] * factor)


def local_large(
    values,
    gates_first,
    gates_second,
    filter_early,
    filter_late,
    skip_early,
    skip_late,
    targets,
    negative_rows,
    recording_ids,
):
    signal = values[0].astype(jnp.float32)
    inner_gate = gates_first[0].astype(jnp.float32)
    outer_gate = gates_second[0].astype(jnp.float32)
    frames = signal.shape[-1]
    early_skip = skip_early[:, None]
    late_skip = skip_late[:, None]
    target_full = targets[0].astype(jnp.float32)
    unit_target = (
        target_full / jnp.sqrt(jnp.sum(target_full * target_full, axis=-1, keepdims=True) + EPSILON)
    ).astype(jnp.bfloat16)
    signal_spec, early_spec = split_pair(signal, filter_early)
    mixed_one = inverse(multiply(signal_spec, early_spec), frames)[0] + early_skip * signal
    hidden = inner_gate * mixed_one
    hidden_spec, late_spec = split_pair(hidden, filter_late)
    mixed_two = inverse(multiply(hidden_spec, late_spec), frames)[0] + late_skip * hidden
    output = outer_gate * mixed_two
    arrived = lax.all_to_all(
        output[None].astype(jnp.bfloat16), "seq", split_axis=2, concat_axis=1, tiled=True
    ).astype(jnp.float32)
    output_rows = jnp.transpose(arrived[0])
    radius = jnp.sqrt(jnp.sum(output_rows * output_rows, axis=-1, keepdims=True) + EPSILON)
    unit_rows = output_rows / radius
    anchors = unit_rows.astype(jnp.bfloat16)
    own_record = lax.axis_index("dp")
    record_count = recording_ids.shape[0]
    record_range = jnp.arange(record_count, dtype=jnp.int32)
    self_label = jnp.sum(jnp.where(record_range == own_record, recording_ids, 0))
    segment = anchors.shape[0]
    block_rows = negative_rows[0]
    block_count = block_rows.shape[0]
    block_size = segment // block_count
    column_ids = jnp.arange(segment, dtype=jnp.int32)
    initial = (
        jnp.zeros((segment,), jnp.float32),
        jnp.zeros((segment, anchors.shape[1]), jnp.float32),
    )
    shard_rows = lax.all_gather(unit_target[None], "dp", axis=0, tiled=True)

    def one_record(partial_value, member):
        pool_rows, record = member
        label = jnp.sum(jnp.where(record_range == record, recording_ids, 0))
        allowed = (label != self_label).astype(jnp.float32)
        matches = (block_rows[:, :, None] == (record * segment + column_ids)[None, None, :]).astype(
            jnp.float32
        )
        counts = jnp.sum(matches, axis=1) * allowed
        counts = jnp.broadcast_to(counts[:, None, :], (block_count, block_size, segment)).reshape(
            segment, segment
        )
        scores = (
            lax.dot_general(
                anchors, pool_rows, (((1,), (1,)), ((), ())), preferred_element_type=jnp.float32
            )
            * INVERSE_TEMP
        )
        weights = counts * jnp.exp(scores)
        numerator = jnp.dot(
            weights.astype(jnp.bfloat16), pool_rows, preferred_element_type=jnp.float32
        )
        return ((partial_value[0] + jnp.sum(weights, axis=-1), partial_value[1] + numerator), None)

    records = jnp.arange(shard_rows.shape[0], dtype=jnp.int32)
    summed = lax.scan(one_record, initial, (shard_rows, records))[0]
    unit_self = unit_target.astype(jnp.float32)
    positive = jnp.exp(jnp.sum(anchors.astype(jnp.float32) * unit_self, axis=-1) * INVERSE_TEMP)
    totals = positive + summed[0]
    anchor_grad = ((positive / totals - 1.0)[:, None] * unit_self + summed[1] / totals[:, None]) * (
        INVERSE_TEMP * LOSS_SCALE
    )
    frame_grad = (
        anchor_grad - unit_rows * jnp.sum(unit_rows * anchor_grad, axis=-1, keepdims=True)
    ) / radius
    arrived_back = lax.all_to_all(
        shortened(jnp.transpose(frame_grad)[None]), "seq", split_axis=1, concat_axis=2, tiled=True
    )
    cotangent = arrived_back[0]
    second_grad = (cotangent * mixed_two).astype(jnp.bfloat16)
    late_drive = cotangent * outer_gate
    back_late = spectrum(late_drive)
    late_pair = combine(
        multiply(back_late, conjugate(late_spec)), multiply(back_late, conjugate(hidden_spec))
    )
    hidden_back, late_update = inverse(late_pair, frames)
    hidden_grad = hidden_back + late_skip * late_drive
    first_grad = (hidden_grad * mixed_one).astype(jnp.bfloat16)
    early_drive = hidden_grad * inner_gate
    back_early = spectrum(early_drive)
    early_pair = combine(
        multiply(back_early, conjugate(early_spec)), multiply(back_early, conjugate(signal_spec))
    )
    signal_back, early_update = inverse(early_pair, frames)
    values_grad = (signal_back + early_skip * early_drive).astype(jnp.bfloat16)
    filter_sums = (
        lax.psum(early_update.astype(jnp.bfloat16), "dp").astype(jnp.float32),
        lax.psum(late_update.astype(jnp.bfloat16), "dp").astype(jnp.float32),
    )
    return (
        values_grad[None],
        first_grad[None],
        second_grad[None],
        filter_sums[0] / frames,
        filter_sums[1] / frames,
    )


def tables(frames):
    odd = 2 * np.arange(frames, dtype=np.int64) + 1
    period = 8 * frames
    circle = 2.0 * np.pi / period * np.arange(period)
    product = odd[:, None] * odd[None, :] % period
    highs, lows = [], []
    for wave in (np.cos(circle), np.sin(circle)):
        wave = wave.astype(np.float32)
        high = wave.astype(BF16)
        low = (wave - high.astype(np.float32)).astype(BF16)
        highs.append(high[product])
        lows.append(low[product])
    half = np.pi * odd / (4.0 * frames)
    turn = np.stack([np.cos(half), np.sin(half)]) / frames
    return np.stack(highs), np.stack(lows), turn.astype(np.float32)


def halves(value):
    high = value.astype(BF16)
    return high, (value - high.astype(F32)).astype(BF16)


def product(parts, table_high, table_low):
    high, low = parts
    total = jnp.dot(high, table_high, preferred_element_type=F32)
    if table_low is not None:
        total += jnp.dot(high, table_low, preferred_element_type=F32)
    if low is not None:
        total += jnp.dot(low, table_high, preferred_element_type=F32)
    return total


def kernel(
    sizes,
    values_hbm, first_hbm, second_hbm, early_hbm, late_hbm, early_skip_hbm, late_skip_hbm,
    targets_hbm, rows_hbm, ids_hbm, high_hbm, low_hbm, turn_hbm,
    values_out, first_out, second_out, early_out, late_out,
    values_ref, first_ref, second_ref, early_ref, late_ref, early_skip_ref, late_skip_ref,
    targets_ref, rows_ref, ids_ref, high_ref, low_ref, turn_ref,
    pool, out_send, out_recv, back_send, back_recv, pair_send, pair_recv, ring_send, ring_recv,
    mixed_one, mixed_two, early_spec, late_spec, signal_spec, hidden_spec, counts_ref,
    load_sem, pool_send_sem, pool_recv_sem, pass_send_sem, pass_recv_sem,
    out_send_sem, out_recv_sem, back_send_sem, back_recv_sem,
    pair_send_sem, pair_recv_sem, ring_send_sem, ring_recv_sem,
    share_send_sem, share_recv_sem, last_send_sem, last_recv_sem,
):
    records, stages = sizes
    chips = records // 2
    me = lax.axis_index("dp")
    here = lax.axis_index("seq")
    chip, core = me // 2, me % 2
    across, along = chip % 2, chip // 2
    partner = chip * 2 + (1 - core)
    x_chip = along * 2 + (1 - across)
    y_chip = (1 - along) * 2 + across
    d_chip = (1 - along) * 2 + (1 - across)
    near = (x_chip, y_chip, d_chip)
    channels, frames = mixed_one.shape
    segment = pool.shape[1]
    depth = pool.shape[2]
    part = segment // 2

    barrier = pltpu.get_barrier_semaphore()
    peers = [(partner, here)] + [(c * 2 + core, here) for c in near]
    peers += [(me, lax.rem(here + k, stages)) for k in range(1, stages)]
    for peer in peers:
        pl.semaphore_signal(barrier, inc=1, device_id=peer, device_id_type=MESH)

    loads = {
        name: pltpu.make_async_copy(source, target, load_sem.at[i])
        for i, (name, source, target) in enumerate((
            ("targets", targets_hbm.at[0], targets_ref),
            ("early", early_hbm, early_ref),
            ("high", high_hbm, high_ref),
            ("low", low_hbm, low_ref),
            ("late", late_hbm, late_ref),
            ("turn", turn_hbm, turn_ref),
            ("values", values_hbm.at[0], values_ref),
            ("first", first_hbm.at[0], first_ref),
            ("second", second_hbm.at[0], second_ref),
            ("early_skip", early_skip_hbm, early_skip_ref),
            ("late_skip", late_skip_hbm, late_skip_ref),
            ("rows", rows_hbm.at[0], rows_ref),
            ("ids", ids_hbm, ids_ref),
        ))
    }
    for load in loads.values():
        load.start()

    def remote(source, target, send, recv, device):
        return pltpu.make_async_remote_copy(
            src_ref=source, dst_ref=target, send_sem=send, recv_sem=recv,
            device_id=device, device_id_type=MESH,
        )

    loads["targets"].wait()
    full = targets_ref[...].astype(F32)
    norm = jnp.sqrt(jnp.sum(full * full, axis=-1, keepdims=True) + EPSILON)
    pool[me] = (full / norm).astype(BF16)
    pl.semaphore_wait(barrier, len(peers))

    def piece(owner, h):
        return pool.at[owner * 2 + core, pl.ds(h * part, part)]

    def pool_copy(n):
        owner, h, to = (
            (chip, 1, x_chip), (chip, 0, y_chip), (chip, 0, x_chip), (chip, 1, y_chip),
            (y_chip, 0, x_chip), (x_chip, 1, y_chip),
        )[n]
        block = piece(owner, h)
        return remote(
            block, block, pool_send_sem.at[n], pool_recv_sem.at[n], (to * 2 + core, here)
        )

    def pool_arrival(n):
        owner, h, to = (
            (x_chip, 1, x_chip), (y_chip, 0, y_chip), (x_chip, 0, x_chip), (y_chip, 1, y_chip),
            (d_chip, 0, x_chip), (d_chip, 1, y_chip),
        )[n]
        block = piece(owner, h)
        return remote(
            block, block, pool_send_sem.at[n], pool_recv_sem.at[n], (to * 2 + core, here)
        )

    def passed(n, lane):
        if n == 6:
            block = pool.at[chip * 2 + lane]
        else:
            owner, h = (
                (x_chip, 1), (y_chip, 0), (x_chip, 0), (y_chip, 1), (d_chip, 0), (d_chip, 1)
            )[n]
            block = pool.at[owner * 2 + lane, pl.ds(h * part, part)]
        return remote(block, block, pass_send_sem.at[n], pass_recv_sem.at[n], (partner, here))

    def pass_copy(n):
        return passed(n, core)

    def pass_arrival(n):
        return passed(n, 1 - core)

    for n in range(4):
        pool_copy(n).start()
    pass_copy(6).start()

    def forward(parts):
        return tuple(product(parts, high_ref[i], low_ref[i]) for i in (0, 1))

    def inverse(cosine, sine, fine=True):
        total = None
        for i, wave in enumerate((cosine, sine)):
            part = product((wave.astype(BF16), None), high_ref[i], low_ref[i] if fine else None)
            total = part if total is None else total + part
        return total

    def unshifted(spec):
        cosine, sine = spec
        turn_cosine = turn_ref[0:1, :]
        turn_sine = turn_ref[1:2, :]
        return (
            cosine * turn_cosine + sine * turn_sine,
            sine * turn_cosine - cosine * turn_sine,
        )

    def keep(ref, spec):
        ref[0] = spec[0]
        ref[1] = spec[1]

    def convolved(spec, ref):
        cosine, sine = spec
        return inverse(cosine * ref[0] - sine * ref[1], cosine * ref[1] + sine * ref[0])

    def correlated(spec, ref, fine=True):
        cosine, sine = spec
        return inverse(cosine * ref[0] + sine * ref[1], sine * ref[0] - cosine * ref[1], fine)

    def column(row):
        return jnp.broadcast_to(row, (8, channels)).T[:, 0:1]

    for name in ("early", "high", "low", "turn"):
        loads[name].wait()
    keep(early_spec, unshifted(forward(halves(early_ref[...]))))
    loads["late"].wait()
    keep(late_spec, unshifted(forward(halves(late_ref[...]))))
    for name in ("values", "early_skip", "late_skip"):
        loads[name].wait()
    early_skip = column(early_skip_ref[...])
    late_skip = column(late_skip_ref[...])
    spec = forward((values_ref[...], None))
    mixed_one[...] = convolved(spec, early_spec) + early_skip * values_ref[...].astype(F32)
    signal_waves = spec
    loads["first"].wait()
    hidden = first_ref[...].astype(F32) * mixed_one[...]
    spec = forward((hidden.astype(BF16), None))
    mixed_two[...] = convolved(spec, late_spec) + late_skip * hidden

    loads["second"].wait()
    output = second_ref[...].astype(F32) * mixed_two[...]
    for s in range(stages):
        out_send[s] = output[:, s * segment : (s + 1) * segment].astype(BF16)

    def exchange(k, send, recv, send_sem, recv_sem):
        peer = lax.rem(here + k, stages)
        return remote(send.at[peer], recv.at[here], send_sem.at[k], recv_sem.at[k], (me, peer))

    def exchange_arrival(k, send, recv, send_sem, recv_sem):
        peer = lax.rem(here + stages - k, stages)
        return remote(send.at[peer], recv.at[peer], send_sem.at[k], recv_sem.at[k], (me, peer))

    out_group = (out_send, out_recv, out_send_sem, out_recv_sem)
    back_group = (back_send, back_recv, back_send_sem, back_recv_sem)
    for k in range(1, stages):
        exchange(k, *out_group).start()
    out_recv[here] = out_send[here]

    pool_arrival(1).wait_recv()
    pool_copy(4).start()
    pass_copy(1).start()
    pool_arrival(0).wait_recv()
    pool_copy(5).start()
    pass_copy(0).start()

    keep(signal_spec, unshifted(signal_waves))
    keep(hidden_spec, unshifted(spec))

    loads["rows"].wait()
    loads["ids"].wait()
    blocks = rows_ref.shape[0]
    draws = rows_ref.shape[1]
    block_size = segment // blocks
    frame_block = lax.broadcasted_iota(jnp.int32, (draws, segment), 1) // block_size
    counts = jnp.zeros((records * segment, segment), F32)
    position = lax.broadcasted_iota(jnp.int32, (records * segment, draws), 0)
    for b in range(blocks):
        matches = jnp.where(position == rows_ref[b : b + 1, :], 1.0, 0.0).astype(BF16)
        chosen = jnp.where(frame_block == b, 1.0, 0.0).astype(BF16)
        counts += jnp.dot(matches, chosen, preferred_element_type=F32)
    for c in range(chips):
        counts_ref[c] = counts[c * 2 * segment : (c + 1) * 2 * segment, :]

    self_units = pool[me].astype(F32).T

    for n in (2, 3):
        pool_arrival(n).wait_recv()
        pass_copy(n).start()

    for k in range(1, stages):
        exchange_arrival(k, *out_group).wait_recv()
    rows = jnp.concatenate([out_recv[s] for s in range(stages)], axis=0).astype(F32)
    radius = jnp.sqrt(jnp.sum(rows * rows, axis=0, keepdims=True) + EPSILON)
    unit_rows = rows / radius
    anchors = unit_rows.astype(BF16)
    positive = jnp.exp(jnp.sum(anchors.astype(F32) * self_units, axis=0, keepdims=True) * INVERSE_TEMP)

    upper = lax.broadcasted_iota(jnp.int32, (2 * segment, 1), 0) < segment

    def against(c):
        units = pool[pl.ds(c * 2, 2)].reshape(2 * segment, depth)
        own_id = ids_ref[me]
        allowed = [jnp.where(ids_ref[c * 2 + i] != own_id, 1.0, 0.0).astype(F32) for i in (0, 1)]
        scores = jnp.dot(units, anchors, preferred_element_type=F32) * INVERSE_TEMP
        weights = counts_ref[c] * jnp.where(upper, allowed[0], allowed[1]) * jnp.exp(scores)
        return (
            jnp.sum(weights, axis=0, keepdims=True),
            jnp.dot(weights.T.astype(BF16), units, preferred_element_type=F32),
        )

    pass_arrival(6).wait_recv()
    summed, numerator = against(chip)
    totals = positive + summed
    for c, pieces in ((x_chip, (0, 2)), (y_chip, (1, 3)), (d_chip, (4, 5))):
        if pieces == (4, 5):
            for n in pieces:
                pool_arrival(n).wait_recv()
                pass_copy(n).start()
        for n in pieces:
            pass_arrival(n).wait_recv()
        summed, partial = against(c)
        totals += summed
        numerator += partial
    anchor_grad = ((positive / totals - 1.0) * self_units + numerator.T / totals) * (
        INVERSE_TEMP * LOSS_SCALE
    )
    frame_grad = (
        anchor_grad - unit_rows * jnp.sum(unit_rows * anchor_grad, axis=0, keepdims=True)
    ) / radius
    for s in range(stages):
        back_send[s] = frame_grad[s * channels : (s + 1) * channels, :].astype(BF16)
    for k in range(1, stages):
        exchange(k, *back_group).start()
    back_recv[here] = back_send[here]
    for k in range(1, stages):
        exchange_arrival(k, *back_group).wait_recv()

    half = channels // 2
    shard = half // chips

    def pair_copy(which, lane):
        return remote(
            pair_send.at[which, lane], pair_recv.at[which],
            pair_send_sem.at[which], pair_recv_sem.at[which], (partner, here),
        )

    def spread(which, update):
        for i in (0, 1):
            pair_send[which, i] = update[i * half : (i + 1) * half, :].astype(BF16)
        pair_copy(which, 1 - core).start()

    def ring_copy(which, n):
        return remote(
            ring_send.at[which, near[n]], ring_recv.at[which, n],
            ring_send_sem.at[which, n], ring_recv_sem.at[which, n], (near[n] * 2 + core, here),
        )

    def gather(which):
        pair_copy(which, core).wait_recv()
        joined = pair_send[which, core].astype(F32) + pair_recv[which].astype(F32)
        for j in range(chips):
            ring_send[which, j] = joined[j * shard : (j + 1) * shard, :].astype(BF16)
        for n in (2, 0, 1):
            ring_copy(which, n).start()

    def share_copy(which, target, n):
        block = target.at[core * chips + chip]
        return remote(
            block, block, share_send_sem.at[which, n], share_recv_sem.at[which, n],
            (near[n] * 2 + core, here),
        )

    def share_arrival(which, target, n):
        block = target.at[core * chips + near[n]]
        return remote(
            block, block, share_send_sem.at[which, n], share_recv_sem.at[which, n],
            (near[n] * 2 + core, here),
        )

    sources = near + (chip,)

    def last_copy(which, target, n):
        block = target.at[core * chips + sources[n]]
        return remote(
            block, block, last_send_sem.at[which, n], last_recv_sem.at[which, n], (partner, here)
        )

    def last_arrival(which, target, n):
        block = target.at[(1 - core) * chips + sources[n]]
        return remote(
            block, block, last_send_sem.at[which, n], last_recv_sem.at[which, n], (partner, here)
        )

    def share(which, target):
        total = ring_send[which, chip].astype(F32)
        for n in range(3):
            ring_copy(which, n).wait_recv()
            total += ring_recv[which, n].astype(F32)
        target[core * chips + chip] = total.astype(BF16)
        for n in (2, 0, 1):
            share_copy(which, target, n).start()
        last_copy(which, target, 3).start()

    def relay(which, target):
        for n in range(3):
            share_arrival(which, target, n).wait_recv()
            last_copy(which, target, n).start()

    cotangent = jnp.concatenate([back_recv[s] for s in range(stages)], axis=1).astype(F32)
    late_drive = cotangent * second_ref[...].astype(F32)
    spec = forward((late_drive.astype(BF16), None))
    hidden_grad = correlated(spec, late_spec) + late_skip * late_drive
    spread(1, correlated(spec, hidden_spec, fine=False))
    early_drive = hidden_grad * first_ref[...].astype(F32)
    spec = forward((early_drive.astype(BF16), None))
    spread(0, correlated(spec, signal_spec, fine=False))
    gather(1)
    second_out[0] = (cotangent * mixed_two[...]).astype(BF16)
    first_out[0] = (hidden_grad * mixed_one[...]).astype(BF16)
    gather(0)
    values_out[0] = (correlated(spec, early_spec) + early_skip * early_drive).astype(BF16)
    share(1, late_out)
    share(0, early_out)
    relay(1, late_out)
    relay(0, early_out)

    for n in range(6):
        pool_copy(n).wait_send()
    for n in range(7):
        pass_copy(n).wait_send()
    for k in range(1, stages):
        exchange(k, *out_group).wait_send()
        exchange(k, *back_group).wait_send()
    for which, target in ((1, late_out), (0, early_out)):
        pair_copy(which, 1 - core).wait_send()
        for n in range(3):
            ring_copy(which, n).wait_send()
            share_copy(which, target, n).wait_send()
        for n in range(4):
            last_copy(which, target, n).wait_send()
            last_arrival(which, target, n).wait_recv()


def finish(
    frames, values_in, first_in, second_in, early_in, late_in,
    values_out, first_out, second_out, early_out, late_out, early_wide, late_wide, sems,
):
    copies = [
        pltpu.make_async_copy(source, target, sems.at[i])
        for i, (source, target) in enumerate((
            (values_in, values_out), (first_in, first_out), (second_in, second_out),
            (early_wide, early_out), (late_wide, late_out),
        ))
    ]
    for copy in copies[:3]:
        copy.start()
    late_wide[...] = late_in[...].astype(F32) / frames
    copies[4].start()
    early_wide[...] = early_in[...].astype(F32) / frames
    copies[3].start()
    for copy in copies:
        copy.wait()


def local(
    records, stages,
    values, gates_first, gates_second, filter_early, filter_late, skip_early, skip_late,
    targets, negative_rows, recording_ids,
):
    _, channels, frames = values.shape
    _, segment, depth = targets.shape
    if 8 * frames * frames > TABLE_BYTES or records != 2 * GRID_CHIPS:
        return local_large(
            values, gates_first, gates_second, filter_early, filter_late, skip_early, skip_late,
            targets, negative_rows, recording_ids,
        )
    high, low, turn = tables(frames)
    chips = records // 2
    half = channels // 2
    shard = half // chips
    blocks, draws = negative_rows.shape[1:]
    vmem = pl.BlockSpec(memory_space=pltpu.VMEM)
    hbm = pl.BlockSpec(memory_space=pltpu.HBM)
    stream = pltpu.VMEM(values.shape, BF16)
    update = pltpu.VMEM((records, shard, frames), BF16)
    exchange = pltpu.VMEM((stages, channels, segment), BF16)
    plane = pltpu.VMEM((channels, frames), F32)
    narrow = pltpu.VMEM((channels, frames), BF16)
    spec = pltpu.VMEM((2, channels, frames), F32)
    skip = pltpu.VMEM((1, channels), F32)
    table = pltpu.VMEM(high.shape, BF16)
    semaphores = pltpu.SemaphoreType.DMA
    results = pl.pallas_call(
        functools.partial(kernel, (records, stages)),
        out_shape=(stream, stream, stream, update, update),
        in_specs=[hbm] * 13,
        out_specs=(vmem,) * 5,
        scratch_shapes=[
            narrow, narrow, narrow, plane, plane, skip, skip,
            pltpu.VMEM((segment, depth), BF16), pltpu.VMEM((blocks, draws), jnp.int32),
            pltpu.SMEM((records,), jnp.int32), table, table, pltpu.VMEM(turn.shape, F32),
            pltpu.VMEM((records, segment, depth), BF16),
            exchange, exchange, exchange, exchange,
            pltpu.VMEM((2, 2, half, frames), BF16), pltpu.VMEM((2, half, frames), BF16),
            pltpu.VMEM((2, chips, shard, frames), BF16), pltpu.VMEM((2, 3, shard, frames), BF16),
            plane, plane, spec, spec, spec, spec,
            pltpu.VMEM((chips, 2 * segment, segment), F32),
            semaphores((13,)), semaphores((6,)), semaphores((6,)), semaphores((7,)), semaphores((7,)),
            semaphores((stages,)), semaphores((stages,)), semaphores((stages,)), semaphores((stages,)),
            semaphores((2,)), semaphores((2,)), semaphores((2, 3)), semaphores((2, 3)),
            semaphores((2, 3)), semaphores((2, 3)), semaphores((2, 4)), semaphores((2, 4)),
        ],
        compiler_params=pltpu.CompilerParams(
            collective_id=0, has_side_effects=True, vmem_limit_bytes=VMEM_BYTES
        ),
    )(*(
        pltpu.with_memory_space_constraint(operand, pltpu.HBM)
        for operand in (
            values, gates_first, gates_second, filter_early, filter_late,
            skip_early[None], skip_late[None], targets, negative_rows, recording_ids,
            jnp.asarray(high), jnp.asarray(low), jnp.asarray(turn),
        )
    ))
    wide = (records, shard, frames)
    *streams, early, late = pl.pallas_call(
        functools.partial(finish, frames),
        out_shape=(jax.ShapeDtypeStruct(values.shape, BF16),) * 3 + (jax.ShapeDtypeStruct(wide, F32),) * 2,
        in_specs=[vmem] * 5,
        out_specs=(hbm,) * 5,
        scratch_shapes=[pltpu.VMEM(wide, F32), pltpu.VMEM(wide, F32), semaphores((5,))],
        compiler_params=pltpu.CompilerParams(vmem_limit_bytes=VMEM_BYTES),
    )(*results)
    return (*streams, early.reshape(channels, frames), late.reshape(channels, frames))


def solution(mesh):
    placed = (
        P("dp", "seq", None),
        P("dp", "seq", None),
        P("dp", "seq", None),
        P("seq", None),
        P("seq", None),
        P("seq"),
        P("seq"),
        P("dp", "seq", None),
        P("dp", "seq", None),
        P(),
    )
    return jax.shard_map(
        functools.partial(local, mesh.shape["dp"], mesh.shape["seq"]),
        mesh=mesh,
        in_specs=placed,
        out_specs=(
            P("dp", "seq", None),
            P("dp", "seq", None),
            P("dp", "seq", None),
            P("seq", None),
            P("seq", None),
        ),
        check_vma=False,
    )
```

```python
import functools
import math

import jax
import jax.numpy as jnp
import numpy as np
from jax import lax
from jax.experimental import pallas as pl
from jax.experimental.pallas import tpu as pltpu
from jax.sharding import PartitionSpec as P

EPSILON = 1e-06
INVERSE_TEMP = 10.0
LOSS_SCALE = 256.0
MESH = pl.DeviceIdType.MESH
F32 = jnp.float32
BF16 = jnp.bfloat16
TABLE_BYTES = 16 * 1024 * 1024
INNER_WIDTH = 128
GRID_CHIPS = 4
CHUNKS = 2
VMEM_BYTES = 40 * 1024 * 1024
HIGHEST = lax.Precision.HIGHEST


def shortened(value):

    def short(part):
        return part.astype(jnp.bfloat16) if part.dtype == jnp.float32 else part

    return jax.tree.map(short, value)


def twiddle(row_count, column_count, length, direction):
    product = (
        jnp.arange(row_count, dtype=jnp.int32)[:, None]
        * jnp.arange(column_count, dtype=jnp.int32)[None, :]
        % length
    )
    angles = direction * 2.0 * math.pi / length * product.astype(jnp.float32)
    return (jnp.cos(angles), jnp.sin(angles))


def complex_table(cosines, sines, with_imaginary):
    upper = jnp.concatenate([cosines, sines], axis=1)
    if not with_imaginary:
        return upper
    lower = jnp.concatenate([-sines, cosines], axis=1)
    return jnp.concatenate([upper, lower], axis=0)


def transform(real_part, imaginary, direction, length):
    used = real_part.shape[-1]
    with_imaginary = imaginary is not None
    outer_size = length // INNER_WIDTH
    used_rows = used // INNER_WIDTH
    lead = real_part.shape[:-1]
    folded_real = real_part.reshape(lead + (used_rows, INNER_WIDTH))
    cosines, sines = twiddle(used_rows, outer_size, outer_size, direction)
    table = complex_table(cosines, sines, with_imaginary)
    if with_imaginary:
        stacked = jnp.concatenate(
            [folded_real, imaginary.reshape(lead + (used_rows, INNER_WIDTH))], axis=-2
        )
    else:
        stacked = folded_real
    section = jnp.einsum("...ab,ak->...kb", stacked, table, precision=HIGHEST)
    section_real = section[..., :outer_size, :]
    section_imaginary = section[..., outer_size:, :]
    turn_cosine, turn_sine = twiddle(outer_size, INNER_WIDTH, length, direction)
    turned_real = section_real * turn_cosine - section_imaginary * turn_sine
    turned_imaginary = section_real * turn_sine + section_imaginary * turn_cosine
    inner_cosine, inner_sine = twiddle(INNER_WIDTH, INNER_WIDTH, INNER_WIDTH, direction)
    inner_table = complex_table(inner_cosine, inner_sine, True)
    second = jnp.einsum(
        "...ab,bk->...ak",
        jnp.concatenate([turned_real, turned_imaginary], axis=-1),
        inner_table,
        precision=HIGHEST,
    )
    final_real = jnp.swapaxes(second[..., :INNER_WIDTH], -1, -2).reshape(lead + (length,))
    final_imaginary = jnp.swapaxes(second[..., INNER_WIDTH:], -1, -2).reshape(lead + (length,))
    return (final_real, final_imaginary)


def spectrum(signal):
    return transform(signal, None, -1.0, 2 * signal.shape[-1])


def split_pair(first_signal, second_signal):
    spec_real, spec_imaginary = transform(
        first_signal, second_signal, -1.0, 2 * first_signal.shape[-1]
    )
    mirror_real = jnp.roll(jnp.flip(spec_real, -1), 1, -1)
    mirror_imaginary = jnp.roll(jnp.flip(spec_imaginary, -1), 1, -1)
    first_spec = ((spec_real + mirror_real) * 0.5, (spec_imaginary - mirror_imaginary) * 0.5)
    second_spec = ((spec_imaginary + mirror_imaginary) * 0.5, (mirror_real - spec_real) * 0.5)
    return (first_spec, second_spec)


def multiply(left_side, right_side):
    return (
        left_side[0] * right_side[0] - left_side[1] * right_side[1],
        left_side[0] * right_side[1] + left_side[1] * right_side[0],
    )


def conjugate(spec):
    return (spec[0], -spec[1])


def combine(left_side, right_side):
    return (left_side[0] - right_side[1], left_side[1] + right_side[0])


def inverse(spec, frames):
    length = spec[0].shape[-1]
    out_real, out_imaginary = transform(spec[0], spec[1], 1.0, length)
    factor = 1.0 / length
    return (out_real[..., :frames] * factor, out_imaginary[..., :frames] * factor)


def local_large(
    values,
    gates_first,
    gates_second,
    filter_early,
    filter_late,
    skip_early,
    skip_late,
    targets,
    negative_rows,
    recording_ids,
):
    signal = values[0].astype(jnp.float32)
    inner_gate = gates_first[0].astype(jnp.float32)
    outer_gate = gates_second[0].astype(jnp.float32)
    frames = signal.shape[-1]
    early_skip = skip_early[:, None]
    late_skip = skip_late[:, None]
    target_full = targets[0].astype(jnp.float32)
    unit_target = (
        target_full / jnp.sqrt(jnp.sum(target_full * target_full, axis=-1, keepdims=True) + EPSILON)
    ).astype(jnp.bfloat16)
    signal_spec, early_spec = split_pair(signal, filter_early)
    mixed_one = inverse(multiply(signal_spec, early_spec), frames)[0] + early_skip * signal
    hidden = inner_gate * mixed_one
    hidden_spec, late_spec = split_pair(hidden, filter_late)
    mixed_two = inverse(multiply(hidden_spec, late_spec), frames)[0] + late_skip * hidden
    output = outer_gate * mixed_two
    arrived = lax.all_to_all(
        output[None].astype(jnp.bfloat16), "seq", split_axis=2, concat_axis=1, tiled=True
    ).astype(jnp.float32)
    output_rows = jnp.transpose(arrived[0])
    radius = jnp.sqrt(jnp.sum(output_rows * output_rows, axis=-1, keepdims=True) + EPSILON)
    unit_rows = output_rows / radius
    anchors = unit_rows.astype(jnp.bfloat16)
    own_record = lax.axis_index("dp")
    record_count = recording_ids.shape[0]
    record_range = jnp.arange(record_count, dtype=jnp.int32)
    self_label = jnp.sum(jnp.where(record_range == own_record, recording_ids, 0))
    segment = anchors.shape[0]
    block_rows = negative_rows[0]
    block_count = block_rows.shape[0]
    block_size = segment // block_count
    column_ids = jnp.arange(segment, dtype=jnp.int32)
    initial = (
        jnp.zeros((segment,), jnp.float32),
        jnp.zeros((segment, anchors.shape[1]), jnp.float32),
    )
    shard_rows = lax.all_gather(unit_target[None], "dp", axis=0, tiled=True)

    def one_record(partial_value, member):
        pool_rows, record = member
        label = jnp.sum(jnp.where(record_range == record, recording_ids, 0))
        allowed = (label != self_label).astype(jnp.float32)
        matches = (block_rows[:, :, None] == (record * segment + column_ids)[None, None, :]).astype(
            jnp.float32
        )
        counts = jnp.sum(matches, axis=1) * allowed
        counts = jnp.broadcast_to(counts[:, None, :], (block_count, block_size, segment)).reshape(
            segment, segment
        )
        scores = (
            lax.dot_general(
                anchors, pool_rows, (((1,), (1,)), ((), ())), preferred_element_type=jnp.float32
            )
            * INVERSE_TEMP
        )
        weights = counts * jnp.exp(scores)
        numerator = jnp.dot(
            weights.astype(jnp.bfloat16), pool_rows, preferred_element_type=jnp.float32
        )
        return ((partial_value[0] + jnp.sum(weights, axis=-1), partial_value[1] + numerator), None)

    records = jnp.arange(shard_rows.shape[0], dtype=jnp.int32)
    summed = lax.scan(one_record, initial, (shard_rows, records))[0]
    unit_self = unit_target.astype(jnp.float32)
    positive = jnp.exp(jnp.sum(anchors.astype(jnp.float32) * unit_self, axis=-1) * INVERSE_TEMP)
    totals = positive + summed[0]
    anchor_grad = ((positive / totals - 1.0)[:, None] * unit_self + summed[1] / totals[:, None]) * (
        INVERSE_TEMP * LOSS_SCALE
    )
    frame_grad = (
        anchor_grad - unit_rows * jnp.sum(unit_rows * anchor_grad, axis=-1, keepdims=True)
    ) / radius
    arrived_back = lax.all_to_all(
        shortened(jnp.transpose(frame_grad)[None]), "seq", split_axis=1, concat_axis=2, tiled=True
    )
    cotangent = arrived_back[0]
    second_grad = (cotangent * mixed_two).astype(jnp.bfloat16)
    late_drive = cotangent * outer_gate
    back_late = spectrum(late_drive)
    late_pair = combine(
        multiply(back_late, conjugate(late_spec)), multiply(back_late, conjugate(hidden_spec))
    )
    hidden_back, late_update = inverse(late_pair, frames)
    hidden_grad = hidden_back + late_skip * late_drive
    first_grad = (hidden_grad * mixed_one).astype(jnp.bfloat16)
    early_drive = hidden_grad * inner_gate
    back_early = spectrum(early_drive)
    early_pair = combine(
        multiply(back_early, conjugate(early_spec)), multiply(back_early, conjugate(signal_spec))
    )
    signal_back, early_update = inverse(early_pair, frames)
    values_grad = (signal_back + early_skip * early_drive).astype(jnp.bfloat16)
    filter_sums = (
        lax.psum(early_update.astype(jnp.bfloat16), "dp").astype(jnp.float32),
        lax.psum(late_update.astype(jnp.bfloat16), "dp").astype(jnp.float32),
    )
    return (
        values_grad[None],
        first_grad[None],
        second_grad[None],
        filter_sums[0] / frames,
        filter_sums[1] / frames,
    )


def tables(frames):
    odd = 2 * np.arange(frames, dtype=np.int64) + 1
    period = 8 * frames
    circle = 2.0 * np.pi / period * np.arange(period)
    product = odd[:, None] * odd[None, :] % period
    waves = np.stack([wave.astype(BF16)[product] for wave in (np.cos(circle), np.sin(circle))])
    half = np.pi * odd / (4.0 * frames)
    turn = np.stack([np.cos(half), np.sin(half)]) / frames
    return waves, turn.astype(np.float32)


def kernel(
    sizes,
    values_hbm, first_hbm, second_hbm, early_hbm, late_hbm, early_skip_hbm, late_skip_hbm,
    targets_hbm, rows_hbm, ids_hbm, waves_hbm, turn_hbm,
    values_out, first_out, second_out, early_out, late_out,
    values_ref, first_ref, second_ref, early_ref, late_ref, early_skip_ref, late_skip_ref,
    rows_ref, ids_ref, waves_ref, turn_ref,
    pool, units_ref, out_send, out_recv, back_send, back_recv, pair_send, pair_recv, ring_send, ring_recv,
    mixed_one, mixed_two, early_spec, late_spec, signal_spec, hidden_spec, counts_ref,
    load_sem, pool_send_sem, pool_recv_sem, pass_send_sem, pass_recv_sem,
    out_send_sem, out_recv_sem, back_send_sem, back_recv_sem,
    pair_send_sem, pair_recv_sem, ring_send_sem, ring_recv_sem,
    share_send_sem, share_recv_sem, last_send_sem, last_recv_sem,
):
    records, stages = sizes
    chips = records // 2
    me = lax.axis_index("dp")
    here = lax.axis_index("seq")
    chip, core = me // 2, me % 2
    across, along = chip % 2, chip // 2
    partner = chip * 2 + (1 - core)
    x_chip = along * 2 + (1 - across)
    y_chip = (1 - along) * 2 + across
    d_chip = (1 - along) * 2 + (1 - across)
    near = (x_chip, y_chip, d_chip)
    channels, frames = mixed_one.shape
    segment = pool.shape[1]
    depth = pool.shape[2]
    part = segment // 2

    barrier = pltpu.get_barrier_semaphore()
    peers = [(partner, here)] + [(c * 2 + core, here) for c in near]
    peers += [(me, lax.rem(here + k, stages)) for k in range(1, stages)]
    for peer in peers:
        pl.semaphore_signal(barrier, inc=1, device_id=peer, device_id_type=MESH)

    loads = {
        name: pltpu.make_async_copy(source, target, load_sem.at[i])
        for i, (name, source, target) in enumerate((
            ("early", early_hbm, early_ref),
            ("waves", waves_hbm, waves_ref),
            ("late", late_hbm, late_ref),
            ("turn", turn_hbm, turn_ref),
            ("values", values_hbm.at[0], values_ref),
            ("first", first_hbm.at[0], first_ref),
            ("second", second_hbm.at[0], second_ref),
            ("early_skip", early_skip_hbm, early_skip_ref),
            ("late_skip", late_skip_hbm, late_skip_ref),
            ("rows", rows_hbm.at[0], rows_ref),
            ("ids", ids_hbm, ids_ref),
            ("targets", targets_hbm.at[0], pool.at[me]),
        ))
    }
    for load in loads.values():
        load.start()

    def remote(source, target, send, recv, device):
        return pltpu.make_async_remote_copy(
            src_ref=source, dst_ref=target, send_sem=send, recv_sem=recv,
            device_id=device, device_id_type=MESH,
        )

    pl.semaphore_wait(barrier, len(peers))

    def piece(owner, h):
        return pool.at[owner * 2 + core, pl.ds(h * part, part)]

    def pool_copy(n):
        owner, h, to = (
            (chip, 1, x_chip), (chip, 0, y_chip), (chip, 0, x_chip), (chip, 1, y_chip),
            (y_chip, 0, x_chip), (x_chip, 1, y_chip),
        )[n]
        block = piece(owner, h)
        source = targets_hbm.at[0, pl.ds(h * part, part)] if n < 4 else block
        return remote(
            source, block, pool_send_sem.at[n], pool_recv_sem.at[n], (to * 2 + core, here)
        )

    def pool_arrival(n):
        owner, h, to = (
            (x_chip, 1, x_chip), (y_chip, 0, y_chip), (x_chip, 0, x_chip), (y_chip, 1, y_chip),
            (d_chip, 0, x_chip), (d_chip, 1, y_chip),
        )[n]
        block = piece(owner, h)
        return remote(
            block, block, pool_send_sem.at[n], pool_recv_sem.at[n], (to * 2 + core, here)
        )

    def passed(n, lane):
        if n == 6:
            block = pool.at[chip * 2 + lane]
            return remote(
                targets_hbm.at[0], block, pass_send_sem.at[n], pass_recv_sem.at[n], (partner, here)
            )
        else:
            owner, h = (
                (x_chip, 1), (y_chip, 0), (x_chip, 0), (y_chip, 1), (d_chip, 0), (d_chip, 1)
            )[n]
            block = pool.at[owner * 2 + lane, pl.ds(h * part, part)]
        return remote(block, block, pass_send_sem.at[n], pass_recv_sem.at[n], (partner, here))

    def pass_copy(n):
        return passed(n, core)

    def pass_arrival(n):
        return passed(n, 1 - core)

    for n in range(4):
        pool_copy(n).start()
    pass_copy(6).start()

    def normalize(slot):
        full = pool[slot].astype(F32)
        norm = jnp.sqrt(jnp.sum(full * full, axis=-1, keepdims=True) + EPSILON)
        units_ref[slot] = (full * (1.0 / norm)).astype(BF16)

    def forward(signal):
        signal = signal.astype(BF16)
        return tuple(jnp.dot(signal, waves_ref[i], preferred_element_type=F32) for i in (0, 1))

    def inverse(cosine, sine):
        return jnp.dot(
            cosine.astype(BF16), waves_ref[0], preferred_element_type=F32
        ) + jnp.dot(sine.astype(BF16), waves_ref[1], preferred_element_type=F32)

    def unshifted(spec):
        cosine, sine = spec
        turn_cosine = turn_ref[0:1, :]
        turn_sine = turn_ref[1:2, :]
        return (
            cosine * turn_cosine + sine * turn_sine,
            sine * turn_cosine - cosine * turn_sine,
        )

    def keep(ref, spec):
        ref[0] = spec[0]
        ref[1] = spec[1]

    def convolved(spec, ref):
        cosine, sine = spec
        return inverse(cosine * ref[0] - sine * ref[1], cosine * ref[1] + sine * ref[0])

    def correlated(spec, refs, lines):
        cosine, sine = spec
        waves = []
        for ref in refs:
            real, imaginary = ref[0, lines], ref[1, lines]
            waves.append((cosine * real + sine * imaginary, sine * real - cosine * imaginary))
        joined = inverse(*(jnp.concatenate(wave, axis=0) for wave in zip(*waves)))
        count = joined.shape[0] // len(refs)
        return [joined[i * count : (i + 1) * count] for i in range(len(refs))]

    def column(row):
        return jnp.broadcast_to(row, (8, channels)).T[:, 0:1]

    for name in ("early", "waves", "turn"):
        loads[name].wait()
    keep(early_spec, unshifted(forward(early_ref[...])))
    loads["late"].wait()
    keep(late_spec, unshifted(forward(late_ref[...])))
    for name in ("values", "early_skip", "late_skip"):
        loads[name].wait()
    early_skip = column(early_skip_ref[...])
    late_skip = column(late_skip_ref[...])
    spec = forward(values_ref[...])
    mixed_one[...] = convolved(spec, early_spec) + early_skip * values_ref[...].astype(F32)
    signal_waves = spec
    loads["first"].wait()
    hidden = first_ref[...].astype(F32) * mixed_one[...]
    spec = forward(hidden)
    mixed_two[...] = convolved(spec, late_spec) + late_skip * hidden

    loads["second"].wait()
    output = second_ref[...].astype(F32) * mixed_two[...]
    for s in range(stages):
        out_send[s] = output[:, s * segment : (s + 1) * segment].astype(BF16)

    low_side = 1 - (2 * here) // stages

    def far_peer(j):
        high = stages - 1 - j
        up = high - (here - high + stages) // stages
        down = j + (j - here + stages) // stages
        return low_side * up + (1 - low_side) * down

    def out_copy(peer):
        return remote(
            out_send.at[peer], out_recv.at[here], out_send_sem.at[peer], out_recv_sem.at[here],
            (me, peer),
        )

    def out_arrival(peer):
        return remote(
            out_send.at[peer], out_recv.at[peer], out_send_sem.at[peer], out_recv_sem.at[peer],
            (me, peer),
        )

    def back_copy(j, peer):
        return remote(
            back_send.at[j, peer], back_recv.at[j, here],
            back_send_sem.at[j, peer], back_recv_sem.at[j, here], (me, peer),
        )

    def back_arrival(j, peer):
        return remote(
            back_send.at[j, peer], back_recv.at[j, peer],
            back_send_sem.at[j, peer], back_recv_sem.at[j, peer], (me, peer),
        )

    others = [lax.rem(here + k, stages) for k in range(1, stages)]
    for j in range(stages - 1):
        out_copy(far_peer(j)).start()
    out_recv[here] = out_send[here]

    pool_arrival(1).wait_recv()
    pool_copy(4).start()
    pass_copy(1).start()
    pool_arrival(0).wait_recv()
    pool_copy(5).start()
    pass_copy(0).start()

    keep(signal_spec, unshifted(signal_waves))
    keep(hidden_spec, unshifted(spec))

    loads["rows"].wait()
    loads["ids"].wait()
    blocks = rows_ref.shape[0]
    draws = rows_ref.shape[1]
    block_size = segment // blocks
    frame_block = lax.broadcasted_iota(jnp.int32, (draws, segment), 1) // block_size
    counts = jnp.zeros((records * segment, segment), F32)
    position = lax.broadcasted_iota(jnp.int32, (records * segment, draws), 0)
    for b in range(blocks):
        matches = jnp.where(position == rows_ref[b : b + 1, :], 1.0, 0.0).astype(BF16)
        chosen = jnp.where(frame_block == b, 1.0, 0.0).astype(BF16)
        counts += jnp.dot(matches, chosen, preferred_element_type=F32)
    for c in range(chips):
        counts_ref[c] = counts[c * 2 * segment : (c + 1) * 2 * segment, :]

    loads["targets"].wait()
    normalize(me)
    self_units = units_ref[me].astype(F32).T
    pass_arrival(6).wait_recv()
    normalize(partner)
    for n in (2, 3):
        pool_arrival(n).wait_recv()
        pass_copy(n).start()
    for c in (x_chip, y_chip):
        normalize(c * 2 + core)
    for n in (1, 0, 2, 3):
        pass_arrival(n).wait_recv()
    for c in (x_chip, y_chip):
        normalize(c * 2 + 1 - core)
    for n in (4, 5):
        pool_arrival(n).wait_recv()
        pass_copy(n).start()
    normalize(d_chip * 2 + core)

    for peer in others:
        out_arrival(peer).wait_recv()
    rows = jnp.concatenate([out_recv[s] for s in range(stages)], axis=0).astype(F32)
    radius = jnp.sqrt(jnp.sum(rows * rows, axis=0, keepdims=True) + EPSILON)
    unit_rows = rows * (1.0 / radius)
    anchors = unit_rows.astype(BF16)
    positive = jnp.exp(jnp.sum(anchors.astype(F32) * self_units, axis=0, keepdims=True) * INVERSE_TEMP)
    alignment = jnp.sum(unit_rows * self_units, axis=0, keepdims=True)

    upper = lax.broadcasted_iota(jnp.int32, (2 * segment, 1), 0) < segment

    def against(c):
        units = units_ref[pl.ds(c * 2, 2)].reshape(2 * segment, depth)
        own_id = ids_ref[me]
        allowed = [jnp.where(ids_ref[c * 2 + i] != own_id, 1.0, 0.0).astype(F32) for i in (0, 1)]
        cosines = jnp.dot(units, anchors, preferred_element_type=F32)
        weights = (
            counts_ref[c] * jnp.where(upper, allowed[0], allowed[1]) * jnp.exp(cosines * INVERSE_TEMP)
        )
        rounded = weights.astype(BF16)
        return (
            jnp.sum(weights, axis=0, keepdims=True),
            jnp.sum(rounded.astype(F32) * cosines, axis=0, keepdims=True),
            jnp.dot(weights.T.astype(BF16), units, preferred_element_type=F32),
        )

    summed, turned, numerator = against(chip)
    totals = positive + summed
    for c in (x_chip, y_chip, d_chip):
        if c is d_chip:
            for n in (4, 5):
                pass_arrival(n).wait_recv()
            normalize(c * 2 + 1 - core)
        summed, partial_turned, partial = against(c)
        totals += summed
        turned += partial_turned
        numerator += partial
    scale = INVERSE_TEMP * LOSS_SCALE / radius
    pull = (positive / totals - 1.0) * scale
    push = scale / totals
    tilt = pull * alignment + push * turned
    chunks, _, size, _ = back_recv.shape
    for j in range(chunks):
        for s in range(stages):
            at = slice(s * channels + j * size, s * channels + (j + 1) * size)
            back_send[j, s] = (
                pull * self_units[at] + push * numerator[:, at].T - tilt * unit_rows[at]
            ).astype(BF16)
        for i in range(stages - 1):
            back_copy(j, far_peer(i)).start()
        back_recv[j, here] = back_send[j, here]

    half = size // 2
    shard = half // chips

    def pair_copy(which, j, lane):
        return remote(
            pair_send.at[which, j, lane], pair_recv.at[which, j],
            pair_send_sem.at[which, j], pair_recv_sem.at[which, j], (partner, here),
        )

    def spread(which, j, update):
        for i in (0, 1):
            pair_send[which, j, i] = update[i * half : (i + 1) * half, :].astype(BF16)
        pair_copy(which, j, 1 - core).start()

    def ring_copy(which, j, n):
        return remote(
            ring_send.at[which, j, near[n]], ring_recv.at[which, j, n],
            ring_send_sem.at[which, j, n], ring_recv_sem.at[which, j, n],
            (near[n] * 2 + core, here),
        )

    def gather(which, j):
        pair_copy(which, j, core).wait_recv()
        joined = pair_send[which, j, core].astype(F32) + pair_recv[which, j].astype(F32)
        for c in range(chips):
            ring_send[which, j, c] = joined[c * shard : (c + 1) * shard, :].astype(BF16)
        for n in (2, 0, 1):
            ring_copy(which, j, n).start()

    targets_out = (early_out, late_out)

    def share_copy(which, j, n):
        block = targets_out[which].at[j, core, chip]
        return remote(
            block, block, share_send_sem.at[which, j, n], share_recv_sem.at[which, j, n],
            (near[n] * 2 + core, here),
        )

    def share_arrival(which, j, n):
        block = targets_out[which].at[j, core, near[n]]
        return remote(
            block, block, share_send_sem.at[which, j, n], share_recv_sem.at[which, j, n],
            (near[n] * 2 + core, here),
        )

    sources = near + (chip,)

    def last_copy(which, j, n):
        block = targets_out[which].at[j, core, sources[n]]
        return remote(
            block, block, last_send_sem.at[which, j, n], last_recv_sem.at[which, j, n],
            (partner, here),
        )

    def last_arrival(which, j, n):
        block = targets_out[which].at[j, 1 - core, sources[n]]
        return remote(
            block, block, last_send_sem.at[which, j, n], last_recv_sem.at[which, j, n],
            (partner, here),
        )

    def share(which, j):
        total = ring_send[which, j, chip].astype(F32)
        for n in range(3):
            ring_copy(which, j, n).wait_recv()
            total += ring_recv[which, j, n].astype(F32)
        targets_out[which][j, core, chip] = total.astype(BF16)
        for n in (2, 0, 1):
            share_copy(which, j, n).start()
        last_copy(which, j, 3).start()

    def relay(which, j):
        for n in range(3):
            share_arrival(which, j, n).wait_recv()
            last_copy(which, j, n).start()

    def backward(j):
        for peer in others:
            back_arrival(j, peer).wait_recv()
        lines = slice(j * size, (j + 1) * size)
        cotangent = jnp.concatenate([back_recv[j, s] for s in range(stages)], axis=1).astype(F32)
        late_drive = cotangent * second_ref[lines].astype(F32)
        update, adjoint = correlated(forward(late_drive), (hidden_spec, late_spec), lines)
        spread(1, j, update)
        hidden_grad = adjoint + late_skip[lines] * late_drive
        early_drive = hidden_grad * first_ref[lines].astype(F32)
        update, adjoint = correlated(forward(early_drive), (signal_spec, early_spec), lines)
        spread(0, j, update)
        values_out[0, lines] = (adjoint + early_skip[lines] * early_drive).astype(BF16)
        second_out[0, lines] = (cotangent * mixed_two[lines]).astype(BF16)
        first_out[0, lines] = (hidden_grad * mixed_one[lines]).astype(BF16)

    for j in range(chunks):
        backward(j)
        if j:

            @pl.when(core == 1)
            def _():
                gather(1, j - 1)
                gather(0, j - 1)

        if j + 1 < chunks:

            @pl.when(core == 0)
            def _():
                gather(1, j)
                gather(0, j)

    for which in (1, 0):
        gather(which, chunks - 1)
    for j in range(chunks):
        for which in (1, 0):
            share(which, j)
    for j in range(chunks):
        for which in (1, 0):
            relay(which, j)

    for n in range(6):
        pool_copy(n).wait_send()
    for n in range(7):
        pass_copy(n).wait_send()
    for peer in others:
        out_copy(peer).wait_send()
        for j in range(chunks):
            back_copy(j, peer).wait_send()
    for j in range(chunks):
        for which in (1, 0):
            pair_copy(which, j, 1 - core).wait_send()
            for n in range(3):
                ring_copy(which, j, n).wait_send()
                share_copy(which, j, n).wait_send()
            for n in range(4):
                last_copy(which, j, n).wait_send()
                last_arrival(which, j, n).wait_recv()


def finish(
    frames, values_in, first_in, second_in, early_in, late_in,
    values_out, first_out, second_out, early_out, late_out, early_wide, late_wide, sems,
):
    copies = [
        pltpu.make_async_copy(source, target, sems.at[i])
        for i, (source, target) in enumerate((
            (values_in, values_out), (first_in, first_out), (second_in, second_out),
            (early_wide, early_out), (late_wide, late_out),
        ))
    ]
    for copy in copies[:3]:
        copy.start()
    late_wide[...] = late_in[...].astype(F32) / frames
    copies[4].start()
    early_wide[...] = early_in[...].astype(F32) / frames
    copies[3].start()
    for copy in copies:
        copy.wait()


def local(
    records, stages,
    values, gates_first, gates_second, filter_early, filter_late, skip_early, skip_late,
    targets, negative_rows, recording_ids,
):
    _, channels, frames = values.shape
    _, segment, depth = targets.shape
    if 8 * frames * frames > TABLE_BYTES or records != 2 * GRID_CHIPS:
        return local_large(
            values, gates_first, gates_second, filter_early, filter_late, skip_early, skip_late,
            targets, negative_rows, recording_ids,
        )
    waves, turn = tables(frames)
    chips = records // 2
    size = channels // CHUNKS
    half = size // 2
    shard = half // chips
    blocks, draws = negative_rows.shape[1:]
    vmem = pl.BlockSpec(memory_space=pltpu.VMEM)
    hbm = pl.BlockSpec(memory_space=pltpu.HBM)
    stream = pltpu.VMEM(values.shape, BF16)
    gradient = (CHUNKS, 2, chips, shard, frames)
    update = pltpu.VMEM(gradient, BF16)
    exchange = pltpu.VMEM((stages, channels, segment), BF16)
    plane = pltpu.VMEM((channels, frames), F32)
    narrow = pltpu.VMEM((channels, frames), BF16)
    spec = pltpu.VMEM((2, channels, frames), F32)
    skip = pltpu.VMEM((1, channels), F32)
    back = pltpu.VMEM((CHUNKS, stages, size, segment), BF16)
    semaphores = pltpu.SemaphoreType.DMA
    results = pl.pallas_call(
        functools.partial(kernel, (records, stages)),
        out_shape=(stream, stream, stream, update, update),
        in_specs=[hbm] * 12,
        out_specs=(vmem,) * 5,
        scratch_shapes=[
            narrow, narrow, narrow, plane, plane, skip, skip,
            pltpu.VMEM((blocks, draws), jnp.int32),
            pltpu.SMEM((records,), jnp.int32), pltpu.VMEM(waves.shape, BF16),
            pltpu.VMEM(turn.shape, F32),
            pltpu.VMEM((records, segment, depth), BF16), pltpu.VMEM((records, segment, depth), BF16),
            exchange, exchange, back, back,
            pltpu.VMEM((2, CHUNKS, 2, half, frames), BF16), pltpu.VMEM((2, CHUNKS, half, frames), BF16),
            pltpu.VMEM((2, CHUNKS, chips, shard, frames), BF16),
            pltpu.VMEM((2, CHUNKS, 3, shard, frames), BF16),
            plane, plane, spec, spec, spec, spec,
            pltpu.VMEM((chips, 2 * segment, segment), F32),
            semaphores((12,)), semaphores((6,)), semaphores((6,)), semaphores((7,)), semaphores((7,)),
            semaphores((stages,)), semaphores((stages,)),
            semaphores((CHUNKS, stages)), semaphores((CHUNKS, stages)),
            semaphores((2, CHUNKS)), semaphores((2, CHUNKS)),
            semaphores((2, CHUNKS, 3)), semaphores((2, CHUNKS, 3)),
            semaphores((2, CHUNKS, 3)), semaphores((2, CHUNKS, 3)),
            semaphores((2, CHUNKS, 4)), semaphores((2, CHUNKS, 4)),
        ],
        compiler_params=pltpu.CompilerParams(
            collective_id=0, has_side_effects=True, vmem_limit_bytes=VMEM_BYTES
        ),
    )(*(
        pltpu.with_memory_space_constraint(operand, pltpu.HBM)
        for operand in (
            values, gates_first, gates_second, filter_early, filter_late,
            skip_early[None], skip_late[None], targets, negative_rows, recording_ids,
            jnp.asarray(waves), jnp.asarray(turn),
        )
    ))
    wide = gradient
    *streams, early, late = pl.pallas_call(
        functools.partial(finish, frames),
        out_shape=(jax.ShapeDtypeStruct(values.shape, BF16),) * 3 + (jax.ShapeDtypeStruct(wide, F32),) * 2,
        in_specs=[vmem] * 5,
        out_specs=(hbm,) * 5,
        scratch_shapes=[pltpu.VMEM(wide, F32), pltpu.VMEM(wide, F32), semaphores((5,))],
        compiler_params=pltpu.CompilerParams(vmem_limit_bytes=VMEM_BYTES),
    )(*results)
    return (*streams, early.reshape(channels, frames), late.reshape(channels, frames))


def solution(mesh):
    placed = (
        P("dp", "seq", None),
        P("dp", "seq", None),
        P("dp", "seq", None),
        P("seq", None),
        P("seq", None),
        P("seq"),
        P("seq"),
        P("dp", "seq", None),
        P("dp", "seq", None),
        P(),
    )
    return jax.shard_map(
        functools.partial(local, mesh.shape["dp"], mesh.shape["seq"]),
        mesh=mesh,
        in_specs=placed,
        out_specs=(
            P("dp", "seq", None),
            P("dp", "seq", None),
            P("dp", "seq", None),
            P("seq", None),
            P("seq", None),
        ),
        check_vma=False,
    )
```

```python
import functools
import math

import jax
import jax.numpy as jnp
import numpy as np
from jax import lax
from jax.experimental import pallas as pl
from jax.experimental.pallas import tpu as pltpu
from jax.sharding import PartitionSpec as P

EPSILON = 1e-06
INVERSE_TEMP = 10.0
LOSS_SCALE = 256.0
MESH = pl.DeviceIdType.MESH
F32 = jnp.float32
BF16 = jnp.bfloat16
TABLE_BYTES = 16 * 1024 * 1024
INNER_WIDTH = 128
GRID_CHIPS = 4
CHUNKS = 2
VMEM_BYTES = 40 * 1024 * 1024
HIGHEST = lax.Precision.HIGHEST


def shortened(value):

    def short(part):
        return part.astype(jnp.bfloat16) if part.dtype == jnp.float32 else part

    return jax.tree.map(short, value)


def twiddle(row_count, column_count, length, direction):
    product = (
        jnp.arange(row_count, dtype=jnp.int32)[:, None]
        * jnp.arange(column_count, dtype=jnp.int32)[None, :]
        % length
    )
    angles = direction * 2.0 * math.pi / length * product.astype(jnp.float32)
    return (jnp.cos(angles), jnp.sin(angles))


def complex_table(cosines, sines, with_imaginary):
    upper = jnp.concatenate([cosines, sines], axis=1)
    if not with_imaginary:
        return upper
    lower = jnp.concatenate([-sines, cosines], axis=1)
    return jnp.concatenate([upper, lower], axis=0)


def transform(real_part, imaginary, direction, length):
    used = real_part.shape[-1]
    with_imaginary = imaginary is not None
    outer_size = length // INNER_WIDTH
    used_rows = used // INNER_WIDTH
    lead = real_part.shape[:-1]
    folded_real = real_part.reshape(lead + (used_rows, INNER_WIDTH))
    cosines, sines = twiddle(used_rows, outer_size, outer_size, direction)
    table = complex_table(cosines, sines, with_imaginary)
    if with_imaginary:
        stacked = jnp.concatenate(
            [folded_real, imaginary.reshape(lead + (used_rows, INNER_WIDTH))], axis=-2
        )
    else:
        stacked = folded_real
    section = jnp.einsum("...ab,ak->...kb", stacked, table, precision=HIGHEST)
    section_real = section[..., :outer_size, :]
    section_imaginary = section[..., outer_size:, :]
    turn_cosine, turn_sine = twiddle(outer_size, INNER_WIDTH, length, direction)
    turned_real = section_real * turn_cosine - section_imaginary * turn_sine
    turned_imaginary = section_real * turn_sine + section_imaginary * turn_cosine
    inner_cosine, inner_sine = twiddle(INNER_WIDTH, INNER_WIDTH, INNER_WIDTH, direction)
    inner_table = complex_table(inner_cosine, inner_sine, True)
    second = jnp.einsum(
        "...ab,bk->...ak",
        jnp.concatenate([turned_real, turned_imaginary], axis=-1),
        inner_table,
        precision=HIGHEST,
    )
    final_real = jnp.swapaxes(second[..., :INNER_WIDTH], -1, -2).reshape(lead + (length,))
    final_imaginary = jnp.swapaxes(second[..., INNER_WIDTH:], -1, -2).reshape(lead + (length,))
    return (final_real, final_imaginary)


def spectrum(signal):
    return transform(signal, None, -1.0, 2 * signal.shape[-1])


def split_pair(first_signal, second_signal):
    spec_real, spec_imaginary = transform(
        first_signal, second_signal, -1.0, 2 * first_signal.shape[-1]
    )
    mirror_real = jnp.roll(jnp.flip(spec_real, -1), 1, -1)
    mirror_imaginary = jnp.roll(jnp.flip(spec_imaginary, -1), 1, -1)
    first_spec = ((spec_real + mirror_real) * 0.5, (spec_imaginary - mirror_imaginary) * 0.5)
    second_spec = ((spec_imaginary + mirror_imaginary) * 0.5, (mirror_real - spec_real) * 0.5)
    return (first_spec, second_spec)


def multiply(left_side, right_side):
    return (
        left_side[0] * right_side[0] - left_side[1] * right_side[1],
        left_side[0] * right_side[1] + left_side[1] * right_side[0],
    )


def conjugate(spec):
    return (spec[0], -spec[1])


def combine(left_side, right_side):
    return (left_side[0] - right_side[1], left_side[1] + right_side[0])


def inverse(spec, frames):
    length = spec[0].shape[-1]
    out_real, out_imaginary = transform(spec[0], spec[1], 1.0, length)
    factor = 1.0 / length
    return (out_real[..., :frames] * factor, out_imaginary[..., :frames] * factor)


def local_large(
    values,
    gates_first,
    gates_second,
    filter_early,
    filter_late,
    skip_early,
    skip_late,
    targets,
    negative_rows,
    recording_ids,
):
    signal = values[0].astype(jnp.float32)
    inner_gate = gates_first[0].astype(jnp.float32)
    outer_gate = gates_second[0].astype(jnp.float32)
    frames = signal.shape[-1]
    early_skip = skip_early[:, None]
    late_skip = skip_late[:, None]
    target_full = targets[0].astype(jnp.float32)
    unit_target = (
        target_full / jnp.sqrt(jnp.sum(target_full * target_full, axis=-1, keepdims=True) + EPSILON)
    ).astype(jnp.bfloat16)
    signal_spec, early_spec = split_pair(signal, filter_early)
    mixed_one = inverse(multiply(signal_spec, early_spec), frames)[0] + early_skip * signal
    hidden = inner_gate * mixed_one
    hidden_spec, late_spec = split_pair(hidden, filter_late)
    mixed_two = inverse(multiply(hidden_spec, late_spec), frames)[0] + late_skip * hidden
    output = outer_gate * mixed_two
    arrived = lax.all_to_all(
        output[None].astype(jnp.bfloat16), "seq", split_axis=2, concat_axis=1, tiled=True
    ).astype(jnp.float32)
    output_rows = jnp.transpose(arrived[0])
    radius = jnp.sqrt(jnp.sum(output_rows * output_rows, axis=-1, keepdims=True) + EPSILON)
    unit_rows = output_rows / radius
    anchors = unit_rows.astype(jnp.bfloat16)
    own_record = lax.axis_index("dp")
    record_count = recording_ids.shape[0]
    record_range = jnp.arange(record_count, dtype=jnp.int32)
    self_label = jnp.sum(jnp.where(record_range == own_record, recording_ids, 0))
    segment = anchors.shape[0]
    block_rows = negative_rows[0]
    block_count = block_rows.shape[0]
    block_size = segment // block_count
    column_ids = jnp.arange(segment, dtype=jnp.int32)
    initial = (
        jnp.zeros((segment,), jnp.float32),
        jnp.zeros((segment, anchors.shape[1]), jnp.float32),
    )
    shard_rows = lax.all_gather(unit_target[None], "dp", axis=0, tiled=True)

    def one_record(partial_value, member):
        pool_rows, record = member
        label = jnp.sum(jnp.where(record_range == record, recording_ids, 0))
        allowed = (label != self_label).astype(jnp.float32)
        matches = (block_rows[:, :, None] == (record * segment + column_ids)[None, None, :]).astype(
            jnp.float32
        )
        counts = jnp.sum(matches, axis=1) * allowed
        counts = jnp.broadcast_to(counts[:, None, :], (block_count, block_size, segment)).reshape(
            segment, segment
        )
        scores = (
            lax.dot_general(
                anchors, pool_rows, (((1,), (1,)), ((), ())), preferred_element_type=jnp.float32
            )
            * INVERSE_TEMP
        )
        weights = counts * jnp.exp(scores)
        numerator = jnp.dot(
            weights.astype(jnp.bfloat16), pool_rows, preferred_element_type=jnp.float32
        )
        return ((partial_value[0] + jnp.sum(weights, axis=-1), partial_value[1] + numerator), None)

    records = jnp.arange(shard_rows.shape[0], dtype=jnp.int32)
    summed = lax.scan(one_record, initial, (shard_rows, records))[0]
    unit_self = unit_target.astype(jnp.float32)
    positive = jnp.exp(jnp.sum(anchors.astype(jnp.float32) * unit_self, axis=-1) * INVERSE_TEMP)
    totals = positive + summed[0]
    anchor_grad = ((positive / totals - 1.0)[:, None] * unit_self + summed[1] / totals[:, None]) * (
        INVERSE_TEMP * LOSS_SCALE
    )
    frame_grad = (
        anchor_grad - unit_rows * jnp.sum(unit_rows * anchor_grad, axis=-1, keepdims=True)
    ) / radius
    arrived_back = lax.all_to_all(
        shortened(jnp.transpose(frame_grad)[None]), "seq", split_axis=1, concat_axis=2, tiled=True
    )
    cotangent = arrived_back[0]
    second_grad = (cotangent * mixed_two).astype(jnp.bfloat16)
    late_drive = cotangent * outer_gate
    back_late = spectrum(late_drive)
    late_pair = combine(
        multiply(back_late, conjugate(late_spec)), multiply(back_late, conjugate(hidden_spec))
    )
    hidden_back, late_update = inverse(late_pair, frames)
    hidden_grad = hidden_back + late_skip * late_drive
    first_grad = (hidden_grad * mixed_one).astype(jnp.bfloat16)
    early_drive = hidden_grad * inner_gate
    back_early = spectrum(early_drive)
    early_pair = combine(
        multiply(back_early, conjugate(early_spec)), multiply(back_early, conjugate(signal_spec))
    )
    signal_back, early_update = inverse(early_pair, frames)
    values_grad = (signal_back + early_skip * early_drive).astype(jnp.bfloat16)
    filter_sums = (
        lax.psum(early_update.astype(jnp.bfloat16), "dp").astype(jnp.float32),
        lax.psum(late_update.astype(jnp.bfloat16), "dp").astype(jnp.float32),
    )
    return (
        values_grad[None],
        first_grad[None],
        second_grad[None],
        filter_sums[0] / frames,
        filter_sums[1] / frames,
    )


def tables(frames):
    odd = 2 * np.arange(frames, dtype=np.int64) + 1
    period = 8 * frames
    circle = 2.0 * np.pi / period * np.arange(period)
    product = odd[:, None] * odd[None, :] % period
    waves = np.stack([wave.astype(BF16)[product] for wave in (np.cos(circle), np.sin(circle))])
    half = np.pi * odd / (4.0 * frames)
    turn = np.stack([np.cos(half), np.sin(half)]) / frames
    return waves, turn.astype(np.float32)


def kernel(
    sizes,
    values_hbm, first_hbm, second_hbm, early_hbm, late_hbm, early_skip_hbm, late_skip_hbm,
    targets_hbm, rows_hbm, ids_hbm, waves_hbm, turn_hbm,
    values_out, first_out, second_out, early_out, late_out,
    streams_ref, filters_ref, skips_ref, rows_ref, ids_ref, waves_ref, turn_ref,
    pool, out_send, out_recv, back_send, back_recv, pair_send, pair_recv, ring_send, ring_recv,
    mixed_one, mixed_two, early_spec, late_spec, signal_spec, hidden_spec, drawn_ref,
    load_sem, send_sem, pool_recv_sem, pass_recv_sem, out_recv_sem, back_recv_sem,
    pair_recv_sem, ring_recv_sem, share_recv_sem, last_recv_sem,
):
    records, stages = sizes
    chips = records // 2
    me = lax.axis_index("dp")
    here = lax.axis_index("seq")
    chip, core = me // 2, me % 2
    across, along = chip % 2, chip // 2
    partner = chip * 2 + (1 - core)
    x_chip = along * 2 + (1 - across)
    y_chip = (1 - along) * 2 + across
    d_chip = (1 - along) * 2 + (1 - across)
    near = (x_chip, y_chip, d_chip)
    channels, frames = mixed_one.shape
    segment = pool.shape[1]
    depth = pool.shape[2]
    part = segment // 2

    barrier = pltpu.get_barrier_semaphore()
    peers = [(me, lax.rem(here + k, stages)) for k in range(1, stages)]
    peers += [(c * 2 + core, here) for c in near] + [(partner, here)]
    for peer in peers:
        pl.semaphore_signal(barrier, inc=1, device_id=peer, device_id_type=MESH)

    loads = [
        pltpu.make_async_copy(source, target, load_sem.at[i])
        for i, source, target in (
            (0, early_hbm, filters_ref.at[0]),
            (1, waves_hbm, waves_ref),
            (0, late_hbm, filters_ref.at[1]),
            (2, turn_hbm, turn_ref),
            (3, values_hbm.at[0], streams_ref.at[0]),
            (3, first_hbm.at[0], streams_ref.at[1]),
            (3, second_hbm.at[0], streams_ref.at[2]),
            (4, early_skip_hbm, skips_ref.at[0]),
            (4, late_skip_hbm, skips_ref.at[1]),
            (5, rows_hbm.at[0], rows_ref),
            (6, ids_hbm, ids_ref),
            (7, targets_hbm.at[0], pool.at[me]),
        )
    ]
    for load in loads:
        load.start()

    def loaded(i, ref):
        pltpu.make_async_copy(ref, ref, load_sem.at[i]).wait()

    def remote(source, target, send, recv, device):
        return pltpu.make_async_remote_copy(
            src_ref=source, dst_ref=target, send_sem=send, recv_sem=recv,
            device_id=device, device_id_type=MESH,
        )

    pl.semaphore_wait(barrier, len(peers))

    def sent(ref, sem):
        remote(ref, ref, sem, sem, (partner, here)).wait_send()

    def landed(ref, sem):
        remote(ref, ref, sem, sem, (partner, here)).wait_recv()

    def piece(owner, h):
        return pool.at[owner * 2 + core, pl.ds(h * part, part)]

    def pool_copy(n):
        owner, h, to = (
            (chip, 1, x_chip), (chip, 0, y_chip), (chip, 0, x_chip), (chip, 1, y_chip),
            (y_chip, 0, x_chip), (x_chip, 1, y_chip),
        )[n]
        block = piece(owner, h)
        source = targets_hbm.at[0, pl.ds(h * part, part)] if n < 4 else block
        return remote(
            source, block, send_sem.at[0], pool_recv_sem.at[n], (to * 2 + core, here)
        )

    def pool_arrival(n):
        owner, h, to = (
            (x_chip, 1, x_chip), (y_chip, 0, y_chip), (x_chip, 0, x_chip), (y_chip, 1, y_chip),
            (d_chip, 0, x_chip), (d_chip, 1, y_chip),
        )[n]
        block = piece(owner, h)
        return remote(
            block, block, send_sem.at[0], pool_recv_sem.at[n], (to * 2 + core, here)
        )

    def pass_copy(n):
        if n == 6:
            block = pool.at[me]
            return remote(
                targets_hbm.at[0], block, send_sem.at[1], pass_recv_sem.at[0], (partner, here)
            )
        else:
            owner, h = (
                (x_chip, 1), (y_chip, 0), (x_chip, 0), (y_chip, 1), (d_chip, 0), (d_chip, 1)
            )[n]
            block = piece(owner, h)
        return remote(
            block, block, send_sem.at[1], pass_recv_sem.at[1 + n // 4], (partner, here)
        )

    for n in range(4):
        pool_copy(n).start()
    pass_copy(6).start()

    def normalized(rows):
        norm = jnp.sqrt(jnp.sum(rows * rows, axis=-1, keepdims=True) + EPSILON)
        return (rows * (1.0 / norm)).astype(BF16)

    def forward(signal):
        signal = signal.astype(BF16)
        return tuple(jnp.dot(signal, waves_ref[i], preferred_element_type=F32) for i in (0, 1))

    def inverse(cosine, sine):
        return jnp.dot(
            cosine.astype(BF16), waves_ref[0], preferred_element_type=F32
        ) + jnp.dot(sine.astype(BF16), waves_ref[1], preferred_element_type=F32)

    def unshifted(spec):
        cosine, sine = spec
        turn_cosine = turn_ref[0:1, :]
        turn_sine = turn_ref[1:2, :]
        return (
            cosine * turn_cosine + sine * turn_sine,
            sine * turn_cosine - cosine * turn_sine,
        )

    def keep(ref, spec):
        ref[0] = spec[0]
        ref[1] = spec[1]

    def convolved(spec, ref):
        cosine, sine = spec
        return inverse(cosine * ref[0] - sine * ref[1], cosine * ref[1] + sine * ref[0])

    def correlated(spec, refs, lines):
        cosine, sine = spec
        waves = []
        for ref in refs:
            real, imaginary = ref[0, lines], ref[1, lines]
            waves.append((cosine * real + sine * imaginary, sine * real - cosine * imaginary))
        joined = inverse(*(jnp.concatenate(wave, axis=0) for wave in zip(*waves)))
        count = joined.shape[0] // len(refs)
        return [joined[i * count : (i + 1) * count] for i in range(len(refs))]

    def column(row):
        return jnp.broadcast_to(row, (8, channels)).T[:, 0:1]

    loaded(0, filters_ref)
    loaded(1, waves_ref)
    loaded(2, turn_ref)
    keep(early_spec, unshifted(forward(filters_ref[0])))
    keep(late_spec, unshifted(forward(filters_ref[1])))
    loaded(3, streams_ref)
    loaded(4, skips_ref)
    values_ref, first_ref, second_ref = (streams_ref.at[i] for i in range(3))
    early_skip = column(skips_ref[0])
    late_skip = column(skips_ref[1])
    spec = forward(values_ref[...])
    mixed_one[...] = convolved(spec, early_spec) + early_skip * values_ref[...].astype(F32)
    signal_waves = spec
    hidden = first_ref[...].astype(F32) * mixed_one[...]
    spec = forward(hidden)
    mixed_two[...] = convolved(spec, late_spec) + late_skip * hidden

    output = second_ref[...].astype(F32) * mixed_two[...]
    for s in range(stages):
        out_send[s] = output[:, s * segment : (s + 1) * segment].astype(BF16)

    low_side = 1 - (2 * here) // stages

    def far_peer(j):
        high = stages - 1 - j
        up = high - (here - high + stages) // stages
        down = j + (j - here + stages) // stages
        return low_side * up + (1 - low_side) * down

    def out_copy(peer):
        return remote(
            out_send.at[peer], out_recv.at[here], send_sem.at[2], out_recv_sem.at[0], (me, peer)
        )

    def back_copy(j, peer):
        return remote(
            back_send.at[j, peer], back_recv.at[j, here],
            send_sem.at[3 + j], back_recv_sem.at[j], (me, peer),
        )

    for j in range(stages - 1):
        out_copy(far_peer(j)).start()
    out_recv[here] = out_send[here]

    pool_arrival(1).wait_recv()
    pool_copy(4).start()
    pass_copy(1).start()
    pool_arrival(0).wait_recv()
    pool_copy(5).start()
    pass_copy(0).start()

    keep(signal_spec, unshifted(signal_waves))
    keep(hidden_spec, unshifted(spec))

    loaded(5, rows_ref)
    loaded(6, ids_ref)
    blocks, draws = rows_ref.shape
    block_size = segment // blocks
    span = drawn_ref.shape[0] // blocks
    place = lax.broadcasted_iota(jnp.int32, (span, draws), 0)
    diagonal = place == lax.broadcasted_iota(jnp.int32, (span, draws), 1)
    padding = lax.broadcasted_iota(jnp.int32, (span, 1), 0) >= draws
    drawn = jnp.concatenate(
        [
            jnp.sum(
                jnp.where(diagonal, rows_ref[b : b + 1, :].astype(F32), 0.0), axis=1, keepdims=True
            )
            - jnp.where(padding, 1.0, 0.0)
            for b in range(blocks)
        ],
        axis=0,
    )
    own_id = ids_ref[me]
    allowed = jnp.zeros_like(drawn)
    for q in range(records):
        inside = (drawn >= q * segment) & (drawn < (q + 1) * segment)
        allowed += jnp.where(inside, jnp.where(ids_ref[q] != own_id, 1.0, 0.0).astype(F32), 0.0)
    grid = (blocks * span, segment)
    row_block = lax.broadcasted_iota(jnp.int32, grid, 0) // span
    frame_block = lax.broadcasted_iota(jnp.int32, grid, 1) // block_size
    mask = jnp.where(row_block == frame_block, allowed, 0.0)
    lane = lax.broadcasted_iota(jnp.int32, (blocks * span, 2 * segment), 1).astype(F32)

    def gathered(c):
        units = pool[pl.ds(c * 2, 2)].reshape(2 * segment, depth)
        first_row = (c * (2 * segment)).astype(F32)
        chosen = jnp.where(drawn - first_row == lane, 1.0, 0.0).astype(BF16)
        return jnp.dot(chosen, units, preferred_element_type=F32)

    loaded(7, pool.at[me])
    self_units = normalized(pool[me].astype(F32)).astype(F32).T
    landed(pool.at[0], pass_recv_sem.at[0])
    drawn_ref[...] = gathered(chip)
    for n in (2, 3, 4, 5):
        pool_arrival(n).wait_recv()
        pass_copy(n).start()
    landed(pool.at[pl.ds(0, 2)], pass_recv_sem.at[1])
    drawn_ref[...] += gathered(x_chip) + gathered(y_chip)

    landed(out_recv.at[pl.ds(0, stages - 1)], out_recv_sem.at[0])
    rows = jnp.concatenate([out_recv[s] for s in range(stages)], axis=0).astype(F32)
    radius = jnp.sqrt(jnp.sum(rows * rows, axis=0, keepdims=True) + EPSILON)
    unit_rows = rows * (1.0 / radius)
    anchors = unit_rows.astype(BF16)
    positive = jnp.exp(jnp.sum(anchors.astype(F32) * self_units, axis=0, keepdims=True) * INVERSE_TEMP)
    alignment = jnp.sum(unit_rows * self_units, axis=0, keepdims=True)

    landed(pool.at[0], pass_recv_sem.at[2])
    negatives = normalized(drawn_ref[...] + gathered(d_chip))
    cosines = jnp.dot(negatives, anchors, preferred_element_type=F32)
    weights = mask * jnp.exp(cosines * INVERSE_TEMP)
    rounded = weights.astype(BF16)
    totals = positive + jnp.sum(weights, axis=0, keepdims=True)
    turned = jnp.sum(rounded.astype(F32) * cosines, axis=0, keepdims=True)
    numerator = jnp.dot(weights.T.astype(BF16), negatives, preferred_element_type=F32)
    scale = INVERSE_TEMP * LOSS_SCALE / radius
    pull = (positive / totals - 1.0) * scale
    push = scale / totals
    tilt = pull * alignment + push * turned
    chunks, _, size, _ = back_recv.shape
    for j in range(chunks):
        for s in range(stages):
            at = slice(s * channels + j * size, s * channels + (j + 1) * size)
            back_send[j, s] = (
                pull * self_units[at] + push * numerator[:, at].T - tilt * unit_rows[at]
            ).astype(BF16)
        if j:
            sent(back_send.at[j - 1, pl.ds(0, stages - 1)], send_sem.at[2 + j])
        for i in range(stages - 1):
            back_copy(j, far_peer(i)).start()
        back_recv[j, here] = back_send[j, here]

    half = size // 2
    shard = half // chips

    def pair_copy(which, j, lane):
        return remote(
            pair_send.at[which, j, lane], pair_recv.at[which, j],
            send_sem.at[3 + chunks], pair_recv_sem.at[which, j], (partner, here),
        )

    def spread(which, j, update):
        for i in (0, 1):
            pair_send[which, j, i] = update[i * half : (i + 1) * half, :].astype(BF16)
        pair_copy(which, j, 1 - core).start()

    def ring_copy(which, j, n):
        return remote(
            ring_send.at[which, j, near[n]], ring_recv.at[which, j, n],
            send_sem.at[4 + chunks], ring_recv_sem.at[which, j], (near[n] * 2 + core, here),
        )

    def gather(which, j):
        landed(pair_recv.at[which, j], pair_recv_sem.at[which, j])
        joined = pair_send[which, j, core].astype(F32) + pair_recv[which, j].astype(F32)
        for c in range(chips):
            ring_send[which, j, c] = joined[c * shard : (c + 1) * shard, :].astype(BF16)
        for n in (2, 0, 1):
            ring_copy(which, j, n).start()

    targets_out = (early_out, late_out)

    def share_copy(which, j, n):
        block = targets_out[which].at[j, core, chip]
        return remote(
            block, block, send_sem.at[5 + chunks], share_recv_sem.at[which, j],
            (near[n] * 2 + core, here),
        )

    def last_copy(which, j, owner):
        block = targets_out[which].at[j, core, owner]
        return remote(
            block, block, send_sem.at[6 + chunks], last_recv_sem.at[0], (partner, here)
        )

    def share(which, j):
        landed(ring_recv.at[which, j], ring_recv_sem.at[which, j])
        total = ring_send[which, j, chip].astype(F32)
        for n in range(3):
            total += ring_recv[which, j, n].astype(F32)
        targets_out[which][j, core, chip] = total.astype(BF16)
        for n in (2, 0, 1):
            share_copy(which, j, n).start()
        last_copy(which, j, chip).start()

    def relay(which, j):
        landed(ring_recv.at[which, j], share_recv_sem.at[which, j])
        for n in range(3):
            last_copy(which, j, near[n]).start()

    def backward(j):
        landed(back_recv.at[j, pl.ds(0, stages - 1)], back_recv_sem.at[j])
        lines = slice(j * size, (j + 1) * size)
        cotangent = jnp.concatenate([back_recv[j, s] for s in range(stages)], axis=1).astype(F32)
        late_drive = cotangent * second_ref[lines].astype(F32)
        update, adjoint = correlated(forward(late_drive), (hidden_spec, late_spec), lines)
        spread(1, j, update)
        hidden_grad = adjoint + late_skip[lines] * late_drive
        early_drive = hidden_grad * first_ref[lines].astype(F32)
        update, adjoint = correlated(forward(early_drive), (signal_spec, early_spec), lines)
        spread(0, j, update)
        values_out[0, lines] = (adjoint + early_skip[lines] * early_drive).astype(BF16)
        second_out[0, lines] = (cotangent * mixed_two[lines]).astype(BF16)
        first_out[0, lines] = (hidden_grad * mixed_one[lines]).astype(BF16)

    for j in range(chunks):
        backward(j)
        for which in (1, 0):
            gather(which, j)
    for j in range(chunks):
        for which in (1, 0):
            share(which, j)
    for j in range(chunks):
        for which in (1, 0):
            relay(which, j)

    sent(pool.at[pl.ds(0, 3)], send_sem.at[0])
    sent(pool.at[pl.ds(0, 4)], send_sem.at[1])
    sent(out_send.at[pl.ds(0, stages - 1)], send_sem.at[2])
    sent(back_send.at[chunks - 1, pl.ds(0, stages - 1)], send_sem.at[2 + chunks])
    sent(pair_recv, send_sem.at[3 + chunks])
    sent(ring_recv, send_sem.at[4 + chunks])
    sent(ring_recv, send_sem.at[5 + chunks])
    sent(pair_recv, send_sem.at[6 + chunks])
    landed(pair_recv, last_recv_sem.at[0])


def finish(
    frames, values_in, first_in, second_in, early_in, late_in,
    values_out, first_out, second_out, early_out, late_out, early_wide, late_wide, sems,
):
    copies = [
        pltpu.make_async_copy(source, target, sems.at[i])
        for i, (source, target) in enumerate((
            (values_in, values_out), (first_in, first_out), (second_in, second_out),
            (early_wide, early_out), (late_wide, late_out),
        ))
    ]
    for copy in copies[:3]:
        copy.start()
    late_wide[...] = late_in[...].astype(F32) / frames
    copies[4].start()
    early_wide[...] = early_in[...].astype(F32) / frames
    copies[3].start()
    for copy in copies:
        copy.wait()


def local(
    records, stages,
    values, gates_first, gates_second, filter_early, filter_late, skip_early, skip_late,
    targets, negative_rows, recording_ids,
):
    _, channels, frames = values.shape
    _, segment, depth = targets.shape
    if 8 * frames * frames > TABLE_BYTES or records != 2 * GRID_CHIPS:
        return local_large(
            values, gates_first, gates_second, filter_early, filter_late, skip_early, skip_late,
            targets, negative_rows, recording_ids,
        )
    waves, turn = tables(frames)
    chips = records // 2
    size = channels // CHUNKS
    half = size // 2
    shard = half // chips
    blocks, draws = negative_rows.shape[1:]
    vmem = pl.BlockSpec(memory_space=pltpu.VMEM)
    hbm = pl.BlockSpec(memory_space=pltpu.HBM)
    stream = pltpu.VMEM(values.shape, BF16)
    gradient = (CHUNKS, 2, chips, shard, frames)
    update = pltpu.VMEM(gradient, BF16)
    exchange = pltpu.VMEM((stages, channels, segment), BF16)
    plane = pltpu.VMEM((channels, frames), F32)
    spec = pltpu.VMEM((2, channels, frames), F32)
    back = pltpu.VMEM((CHUNKS, stages, size, segment), BF16)
    semaphores = pltpu.SemaphoreType.DMA
    results = pl.pallas_call(
        functools.partial(kernel, (records, stages)),
        out_shape=(stream, stream, stream, update, update),
        in_specs=[hbm] * 12,
        out_specs=(vmem,) * 5,
        scratch_shapes=[
            pltpu.VMEM((3, channels, frames), BF16), pltpu.VMEM((2, channels, frames), F32),
            pltpu.VMEM((2, 1, channels), F32), pltpu.VMEM((blocks, draws), jnp.int32),
            pltpu.SMEM((records,), jnp.int32), pltpu.VMEM(waves.shape, BF16),
            pltpu.VMEM(turn.shape, F32),
            pltpu.VMEM((records, segment, depth), BF16),
            exchange, exchange, back, back,
            pltpu.VMEM((2, CHUNKS, 2, half, frames), BF16), pltpu.VMEM((2, CHUNKS, half, frames), BF16),
            pltpu.VMEM((2, CHUNKS, chips, shard, frames), BF16),
            pltpu.VMEM((2, CHUNKS, 3, shard, frames), BF16),
            plane, plane, spec, spec, spec, spec,
            pltpu.VMEM((blocks * -(-draws // 128) * 128, depth), F32),
            semaphores((8,)), semaphores((7 + CHUNKS,)), semaphores((6,)), semaphores((3,)),
            semaphores((1,)), semaphores((CHUNKS,)), semaphores((2, CHUNKS)),
            semaphores((2, CHUNKS)), semaphores((2, CHUNKS)), semaphores((1,)),
        ],
        compiler_params=pltpu.CompilerParams(
            collective_id=0, has_side_effects=True, vmem_limit_bytes=VMEM_BYTES
        ),
    )(*(
        pltpu.with_memory_space_constraint(operand, pltpu.HBM)
        for operand in (
            values, gates_first, gates_second, filter_early, filter_late,
            skip_early[None], skip_late[None], targets, negative_rows, recording_ids,
            jnp.asarray(waves), jnp.asarray(turn),
        )
    ))
    wide = gradient
    *streams, early, late = pl.pallas_call(
        functools.partial(finish, frames),
        out_shape=(jax.ShapeDtypeStruct(values.shape, BF16),) * 3 + (jax.ShapeDtypeStruct(wide, F32),) * 2,
        in_specs=[vmem] * 5,
        out_specs=(hbm,) * 5,
        scratch_shapes=[pltpu.VMEM(wide, F32), pltpu.VMEM(wide, F32), semaphores((5,))],
        compiler_params=pltpu.CompilerParams(vmem_limit_bytes=VMEM_BYTES),
    )(*results)
    return (*streams, early.reshape(channels, frames), late.reshape(channels, frames))


def solution(mesh):
    placed = (
        P("dp", "seq", None),
        P("dp", "seq", None),
        P("dp", "seq", None),
        P("seq", None),
        P("seq", None),
        P("seq"),
        P("seq"),
        P("dp", "seq", None),
        P("dp", "seq", None),
        P(),
    )
    return jax.shard_map(
        functools.partial(local, mesh.shape["dp"], mesh.shape["seq"]),
        mesh=mesh,
        in_specs=placed,
        out_specs=(
            P("dp", "seq", None),
            P("dp", "seq", None),
            P("dp", "seq", None),
            P("seq", None),
            P("seq", None),
        ),
        check_vma=False,
    )
```

```python
import functools
import math

import jax
import jax.numpy as jnp
import numpy as np
from jax import lax
from jax.experimental import pallas as pl
from jax.experimental.pallas import tpu as pltpu
from jax.sharding import PartitionSpec as P

EPSILON = 1e-06
INVERSE_TEMP = 10.0
LOSS_SCALE = 256.0
MESH = pl.DeviceIdType.MESH
F32 = jnp.float32
BF16 = jnp.bfloat16
TABLE_BYTES = 16 * 1024 * 1024
INNER_WIDTH = 128
GRID_CHIPS = 4
FINE_FILTERS = True
FINE_VALUES = True
FINE_HIDDEN = False
CHUNKS = 2
VMEM_BYTES = 40 * 1024 * 1024
HIGHEST = lax.Precision.HIGHEST


def shortened(value):

    def short(part):
        return part.astype(jnp.bfloat16) if part.dtype == jnp.float32 else part

    return jax.tree.map(short, value)


def twiddle(row_count, column_count, length, direction):
    product = (
        jnp.arange(row_count, dtype=jnp.int32)[:, None]
        * jnp.arange(column_count, dtype=jnp.int32)[None, :]
        % length
    )
    angles = direction * 2.0 * math.pi / length * product.astype(jnp.float32)
    return (jnp.cos(angles), jnp.sin(angles))


def complex_table(cosines, sines, with_imaginary):
    upper = jnp.concatenate([cosines, sines], axis=1)
    if not with_imaginary:
        return upper
    lower = jnp.concatenate([-sines, cosines], axis=1)
    return jnp.concatenate([upper, lower], axis=0)


def transform(real_part, imaginary, direction, length):
    used = real_part.shape[-1]
    with_imaginary = imaginary is not None
    outer_size = length // INNER_WIDTH
    used_rows = used // INNER_WIDTH
    lead = real_part.shape[:-1]
    folded_real = real_part.reshape(lead + (used_rows, INNER_WIDTH))
    cosines, sines = twiddle(used_rows, outer_size, outer_size, direction)
    table = complex_table(cosines, sines, with_imaginary)
    if with_imaginary:
        stacked = jnp.concatenate(
            [folded_real, imaginary.reshape(lead + (used_rows, INNER_WIDTH))], axis=-2
        )
    else:
        stacked = folded_real
    section = jnp.einsum("...ab,ak->...kb", stacked, table, precision=HIGHEST)
    section_real = section[..., :outer_size, :]
    section_imaginary = section[..., outer_size:, :]
    turn_cosine, turn_sine = twiddle(outer_size, INNER_WIDTH, length, direction)
    turned_real = section_real * turn_cosine - section_imaginary * turn_sine
    turned_imaginary = section_real * turn_sine + section_imaginary * turn_cosine
    inner_cosine, inner_sine = twiddle(INNER_WIDTH, INNER_WIDTH, INNER_WIDTH, direction)
    inner_table = complex_table(inner_cosine, inner_sine, True)
    second = jnp.einsum(
        "...ab,bk->...ak",
        jnp.concatenate([turned_real, turned_imaginary], axis=-1),
        inner_table,
        precision=HIGHEST,
    )
    final_real = jnp.swapaxes(second[..., :INNER_WIDTH], -1, -2).reshape(lead + (length,))
    final_imaginary = jnp.swapaxes(second[..., INNER_WIDTH:], -1, -2).reshape(lead + (length,))
    return (final_real, final_imaginary)


def spectrum(signal):
    return transform(signal, None, -1.0, 2 * signal.shape[-1])


def split_pair(first_signal, second_signal):
    spec_real, spec_imaginary = transform(
        first_signal, second_signal, -1.0, 2 * first_signal.shape[-1]
    )
    mirror_real = jnp.roll(jnp.flip(spec_real, -1), 1, -1)
    mirror_imaginary = jnp.roll(jnp.flip(spec_imaginary, -1), 1, -1)
    first_spec = ((spec_real + mirror_real) * 0.5, (spec_imaginary - mirror_imaginary) * 0.5)
    second_spec = ((spec_imaginary + mirror_imaginary) * 0.5, (mirror_real - spec_real) * 0.5)
    return (first_spec, second_spec)


def multiply(left_side, right_side):
    return (
        left_side[0] * right_side[0] - left_side[1] * right_side[1],
        left_side[0] * right_side[1] + left_side[1] * right_side[0],
    )


def conjugate(spec):
    return (spec[0], -spec[1])


def combine(left_side, right_side):
    return (left_side[0] - right_side[1], left_side[1] + right_side[0])


def inverse(spec, frames):
    length = spec[0].shape[-1]
    out_real, out_imaginary = transform(spec[0], spec[1], 1.0, length)
    factor = 1.0 / length
    return (out_real[..., :frames] * factor, out_imaginary[..., :frames] * factor)


def local_large(
    values,
    gates_first,
    gates_second,
    filter_early,
    filter_late,
    skip_early,
    skip_late,
    targets,
    negative_rows,
    recording_ids,
):
    signal = values[0].astype(jnp.float32)
    inner_gate = gates_first[0].astype(jnp.float32)
    outer_gate = gates_second[0].astype(jnp.float32)
    frames = signal.shape[-1]
    early_skip = skip_early[:, None]
    late_skip = skip_late[:, None]
    target_full = targets[0].astype(jnp.float32)
    unit_target = (
        target_full / jnp.sqrt(jnp.sum(target_full * target_full, axis=-1, keepdims=True) + EPSILON)
    ).astype(jnp.bfloat16)
    signal_spec, early_spec = split_pair(signal, filter_early)
    mixed_one = inverse(multiply(signal_spec, early_spec), frames)[0] + early_skip * signal
    hidden = inner_gate * mixed_one
    hidden_spec, late_spec = split_pair(hidden, filter_late)
    mixed_two = inverse(multiply(hidden_spec, late_spec), frames)[0] + late_skip * hidden
    output = outer_gate * mixed_two
    arrived = lax.all_to_all(
        output[None].astype(jnp.bfloat16), "seq", split_axis=2, concat_axis=1, tiled=True
    ).astype(jnp.float32)
    output_rows = jnp.transpose(arrived[0])
    radius = jnp.sqrt(jnp.sum(output_rows * output_rows, axis=-1, keepdims=True) + EPSILON)
    unit_rows = output_rows / radius
    anchors = unit_rows.astype(jnp.bfloat16)
    own_record = lax.axis_index("dp")
    record_count = recording_ids.shape[0]
    record_range = jnp.arange(record_count, dtype=jnp.int32)
    self_label = jnp.sum(jnp.where(record_range == own_record, recording_ids, 0))
    segment = anchors.shape[0]
    block_rows = negative_rows[0]
    block_count = block_rows.shape[0]
    block_size = segment // block_count
    column_ids = jnp.arange(segment, dtype=jnp.int32)
    initial = (
        jnp.zeros((segment,), jnp.float32),
        jnp.zeros((segment, anchors.shape[1]), jnp.float32),
    )
    shard_rows = lax.all_gather(unit_target[None], "dp", axis=0, tiled=True)

    def one_record(partial_value, member):
        pool_rows, record = member
        label = jnp.sum(jnp.where(record_range == record, recording_ids, 0))
        allowed = (label != self_label).astype(jnp.float32)
        matches = (block_rows[:, :, None] == (record * segment + column_ids)[None, None, :]).astype(
            jnp.float32
        )
        counts = jnp.sum(matches, axis=1) * allowed
        counts = jnp.broadcast_to(counts[:, None, :], (block_count, block_size, segment)).reshape(
            segment, segment
        )
        scores = (
            lax.dot_general(
                anchors, pool_rows, (((1,), (1,)), ((), ())), preferred_element_type=jnp.float32
            )
            * INVERSE_TEMP
        )
        weights = counts * jnp.exp(scores)
        numerator = jnp.dot(
            weights.astype(jnp.bfloat16), pool_rows, preferred_element_type=jnp.float32
        )
        return ((partial_value[0] + jnp.sum(weights, axis=-1), partial_value[1] + numerator), None)

    records = jnp.arange(shard_rows.shape[0], dtype=jnp.int32)
    summed = lax.scan(one_record, initial, (shard_rows, records))[0]
    unit_self = unit_target.astype(jnp.float32)
    positive = jnp.exp(jnp.sum(anchors.astype(jnp.float32) * unit_self, axis=-1) * INVERSE_TEMP)
    totals = positive + summed[0]
    anchor_grad = ((positive / totals - 1.0)[:, None] * unit_self + summed[1] / totals[:, None]) * (
        INVERSE_TEMP * LOSS_SCALE
    )
    frame_grad = (
        anchor_grad - unit_rows * jnp.sum(unit_rows * anchor_grad, axis=-1, keepdims=True)
    ) / radius
    arrived_back = lax.all_to_all(
        shortened(jnp.transpose(frame_grad)[None]), "seq", split_axis=1, concat_axis=2, tiled=True
    )
    cotangent = arrived_back[0]
    second_grad = (cotangent * mixed_two).astype(jnp.bfloat16)
    late_drive = cotangent * outer_gate
    back_late = spectrum(late_drive)
    late_pair = combine(
        multiply(back_late, conjugate(late_spec)), multiply(back_late, conjugate(hidden_spec))
    )
    hidden_back, late_update = inverse(late_pair, frames)
    hidden_grad = hidden_back + late_skip * late_drive
    first_grad = (hidden_grad * mixed_one).astype(jnp.bfloat16)
    early_drive = hidden_grad * inner_gate
    back_early = spectrum(early_drive)
    early_pair = combine(
        multiply(back_early, conjugate(early_spec)), multiply(back_early, conjugate(signal_spec))
    )
    signal_back, early_update = inverse(early_pair, frames)
    values_grad = (signal_back + early_skip * early_drive).astype(jnp.bfloat16)
    filter_sums = (
        lax.psum(early_update.astype(jnp.bfloat16), "dp").astype(jnp.float32),
        lax.psum(late_update.astype(jnp.bfloat16), "dp").astype(jnp.float32),
    )
    return (
        values_grad[None],
        first_grad[None],
        second_grad[None],
        filter_sums[0] / frames,
        filter_sums[1] / frames,
    )


def tables(frames):
    middle = frames // 2
    order = np.concatenate([np.arange(0, frames, 2), np.arange(1, frames, 2)])
    odd = 2 * order.astype(np.int64) + 1
    product = odd[None, :] * (2 * np.arange(middle, dtype=np.int64) + 1)[:, None]
    angle = np.pi / (4.0 * frames) * (product % (8 * frames))
    plus, minus = np.cos(angle) + np.sin(angle), np.cos(angle) - np.sin(angle)
    even = np.arange(frames) < middle
    ahead = np.stack([np.where(even, plus, minus), np.where(even, minus, plus)]).astype(np.float32)
    half = np.pi * odd / (4.0 * frames)
    both = np.stack([np.cos(half) + np.sin(half), np.cos(half) - np.sin(half)]) / (4.0 * frames)
    turn = np.where(even, both, both[::-1]).astype(np.float32)
    high = ahead.astype(BF16)
    low = (ahead - high.astype(np.float32)).astype(BF16)
    return np.concatenate([high, low]), np.swapaxes(high, 1, 2), turn


def kernel(
    sizes,
    values_hbm, first_hbm, second_hbm, early_hbm, late_hbm, early_skip_hbm, late_skip_hbm,
    targets_hbm, rows_hbm, ids_hbm, waves_hbm, inverse_hbm, turn_hbm,
    values_out, first_out, second_out, early_out, late_out,
    streams_ref, filters_ref, skips_ref, rows_ref, ids_ref, waves_ref, inverse_ref, turn_ref,
    pool, out_send, out_recv, back_send, back_recv, pair_send, pair_recv, ring_send, ring_recv,
    mixed_one, mixed_two, early_spec, late_spec, signal_spec, hidden_spec, drawn_ref,
    load_sem, send_sem, pool_recv_sem, pass_recv_sem, out_recv_sem, back_recv_sem,
    pair_recv_sem, ring_recv_sem, share_recv_sem, last_recv_sem,
):
    records, stages = sizes
    chips = records // 2
    me = lax.axis_index("dp")
    here = lax.axis_index("seq")
    chip, core = me // 2, me % 2
    across, along = chip % 2, chip // 2
    partner = chip * 2 + (1 - core)
    x_chip = along * 2 + (1 - across)
    y_chip = (1 - along) * 2 + across
    d_chip = (1 - along) * 2 + (1 - across)
    near = (x_chip, y_chip, d_chip)
    channels, frames = mixed_one.shape
    segment = pool.shape[1]
    depth = pool.shape[2]
    part = segment // 2

    barrier = pltpu.get_barrier_semaphore()
    peers = [(me, lax.rem(here + k, stages)) for k in range(1, stages)]
    peers += [(c * 2 + core, here) for c in near] + [(partner, here)]
    for peer in peers:
        pl.semaphore_signal(barrier, inc=1, device_id=peer, device_id_type=MESH)

    loads = [
        pltpu.make_async_copy(source, target, load_sem.at[i])
        for i, source, target in (
            (0, early_hbm, filters_ref.at[0]),
            (1, waves_hbm, waves_ref),
            (0, late_hbm, filters_ref.at[1]),
            (2, turn_hbm, turn_ref),
            (3, values_hbm.at[0], streams_ref.at[0]),
            (3, first_hbm.at[0], streams_ref.at[1]),
            (3, second_hbm.at[0], streams_ref.at[2]),
            (4, early_skip_hbm, skips_ref.at[0]),
            (4, late_skip_hbm, skips_ref.at[1]),
            (5, rows_hbm.at[0], rows_ref),
            (6, ids_hbm, ids_ref),
            (7, targets_hbm.at[0], pool.at[me]),
            (8, inverse_hbm, inverse_ref),
        )
    ]
    for load in loads:
        load.start()

    def loaded(i, ref):
        pltpu.make_async_copy(ref, ref, load_sem.at[i]).wait()

    def remote(source, target, send, recv, device):
        return pltpu.make_async_remote_copy(
            src_ref=source, dst_ref=target, send_sem=send, recv_sem=recv,
            device_id=device, device_id_type=MESH,
        )

    pl.semaphore_wait(barrier, len(peers))

    def sent(ref, sem):
        remote(ref, ref, sem, sem, (partner, here)).wait_send()

    def landed(ref, sem):
        remote(ref, ref, sem, sem, (partner, here)).wait_recv()

    def piece(owner, start, count):
        return pool.at[owner * 2 + core, pl.ds(start, count)]

    quarter = part // 2
    whole = ((part, part), (0, part), (0, part), (part, part))
    quarters = ((0, quarter), (part, quarter), (quarter, quarter), (part + quarter, quarter))
    spans = whole + quarters
    lanes = (x_chip, y_chip, x_chip, y_chip) * 2
    origins = (chip,) * 4 + (y_chip, x_chip) * 2
    arrivals = (x_chip, y_chip, x_chip, y_chip) + (d_chip,) * 4

    def pool_copy(n):
        block = piece(origins[n], *spans[n])
        source = targets_hbm.at[0, pl.ds(*spans[n])] if n < 4 else block
        return remote(
            source, block, send_sem.at[0], pool_recv_sem.at[n], (lanes[n] * 2 + core, here)
        )

    def pool_arrival(n):
        block = piece(arrivals[n], *spans[n])
        return remote(
            block, block, send_sem.at[0], pool_recv_sem.at[n], (lanes[n] * 2 + core, here)
        )

    def pass_copy(n):
        block = piece(arrivals[n], *spans[n])
        return remote(
            block, block, send_sem.at[1], pass_recv_sem.at[1 + n // 4], (partner, here)
        )

    for n in range(4):
        pool_copy(n).start()
    remote(
        targets_hbm.at[0], pool.at[me], send_sem.at[1], pass_recv_sem.at[0], (partner, here)
    ).start()

    def normalized(rows):
        norm = jnp.sqrt(jnp.sum(rows * rows, axis=-1, keepdims=True) + EPSILON)
        return (rows * (1.0 / norm)).astype(BF16)

    middle = frames // 2
    flip_row = lax.broadcasted_iota(jnp.int32, (middle, middle), 0)
    flip_column = lax.broadcasted_iota(jnp.int32, (middle, middle), 1)
    mirror = jnp.where(flip_row + flip_column == middle - 1, 1.0, 0.0).astype(BF16)

    def halves(value):
        high = value.astype(BF16)
        return high, (value - high.astype(F32)).astype(BF16)

    def turned_over_wide(signal):
        tail = sum(
            jnp.dot(part, mirror, preferred_element_type=F32)
            for part in halves(signal[:, middle:])
        )
        return jnp.concatenate([signal[:, :middle], tail], axis=1)

    def turned_over(signal):
        signal = signal.astype(BF16)
        tail = jnp.dot(signal[:, middle:], mirror, preferred_element_type=F32).astype(BF16)
        return jnp.concatenate([signal[:, :middle], tail], axis=1)

    def forward(signal, fine=False):
        head, tail = signal[:, :middle].astype(F32), signal[:, middle:].astype(F32)
        spec = []
        for i, fold in enumerate((head + tail, head - tail)):
            high, low = halves(fold)
            wave = jnp.dot(high, waves_ref[i], preferred_element_type=F32)
            if fine:
                wave += jnp.dot(high, waves_ref[2 + i], preferred_element_type=F32)
                wave += jnp.dot(low, waves_ref[i], preferred_element_type=F32)
            spec.append(wave)
        return tuple(spec)

    def inverse(*spec):
        plus, minus = (
            jnp.dot(wave.astype(BF16), inverse_ref[i], preferred_element_type=F32)
            for i, wave in enumerate(spec)
        )
        return jnp.concatenate([plus + minus, plus - minus], axis=1)

    def unshifted(spec):
        first, second = spec
        turn_first = turn_ref[0:1, :]
        turn_second = turn_ref[1:2, :]
        return (
            first * turn_first + second * turn_second,
            first * turn_second - second * turn_first,
        )

    def keep(ref, spec):
        ref[0] = spec[0]
        ref[1] = spec[1]

    def convolved(spec, ref):
        first, second = spec
        return inverse(first * ref[0] + second * ref[1], second * ref[0] - first * ref[1])

    def correlated(spec, refs, lines):
        first, second = spec
        waves = []
        for ref in refs:
            real, imaginary = ref[0, lines], ref[1, lines]
            waves.append((first * real - second * imaginary, second * real + first * imaginary))
        joined = inverse(*(jnp.concatenate(wave, axis=0) for wave in zip(*waves)))
        count = joined.shape[0] // len(refs)
        return [joined[i * count : (i + 1) * count] for i in range(len(refs))]

    def column(row):
        return jnp.broadcast_to(row, (8, channels)).T[:, 0:1]

    loaded(0, filters_ref)
    loaded(1, waves_ref)
    loaded(2, turn_ref)
    keep(early_spec, unshifted(forward(turned_over_wide(filters_ref[0]), FINE_FILTERS)))
    keep(late_spec, unshifted(forward(turned_over_wide(filters_ref[1]), FINE_FILTERS)))
    loaded(3, streams_ref)
    loaded(4, skips_ref)
    values_ref, first_ref, second_ref = (streams_ref.at[i] for i in range(3))
    for ref in (values_ref, first_ref, second_ref):
        ref[...] = turned_over(ref[...])
    loaded(8, inverse_ref)
    early_skip = column(skips_ref[0])
    late_skip = column(skips_ref[1])
    spec = forward(values_ref[...], FINE_VALUES)
    mixed_one[...] = convolved(spec, early_spec) + early_skip * values_ref[...].astype(F32)
    signal_waves = spec
    hidden = first_ref[...].astype(F32) * mixed_one[...]
    spec = forward(hidden, FINE_HIDDEN)
    mixed_two[...] = convolved(spec, late_spec) + late_skip * hidden

    output = second_ref[...].astype(F32) * mixed_two[...]
    order = [s if 2 * s < stages else stages - 1 - s + stages // 2 for s in range(stages)]
    for i, s in enumerate(order):
        out_send[s] = output[:, i * segment : (i + 1) * segment].astype(BF16)

    low_side = 1 - (2 * here) // stages

    def far_peer(j):
        high = stages - 1 - j
        up = high - (here - high + stages) // stages
        down = j + (j - here + stages) // stages
        return low_side * up + (1 - low_side) * down

    def out_copy(peer):
        return remote(
            out_send.at[peer], out_recv.at[here], send_sem.at[2], out_recv_sem.at[0], (me, peer)
        )

    def back_copy(j, peer):
        return remote(
            back_send.at[j, peer], back_recv.at[j, here],
            send_sem.at[3 + j], back_recv_sem.at[j], (me, peer),
        )

    for j in range(stages - 1):
        out_copy(far_peer(j)).start()
    out_recv[here] = out_send[here]

    pool_arrival(1).wait_recv()
    pool_copy(4).start()
    pool_copy(6).start()
    pass_copy(1).start()
    pool_arrival(0).wait_recv()
    pool_copy(5).start()
    pool_copy(7).start()
    pass_copy(0).start()

    keep(signal_spec, unshifted(signal_waves))
    keep(hidden_spec, unshifted(spec))

    loaded(5, rows_ref)
    loaded(6, ids_ref)
    blocks, draws = rows_ref.shape
    block_size = segment // blocks
    span = drawn_ref.shape[0] // blocks
    place = lax.broadcasted_iota(jnp.int32, (span, draws), 0)
    diagonal = place == lax.broadcasted_iota(jnp.int32, (span, draws), 1)
    padding = lax.broadcasted_iota(jnp.int32, (span, 1), 0) >= draws
    drawn = jnp.concatenate(
        [
            jnp.sum(
                jnp.where(diagonal, rows_ref[b : b + 1, :].astype(F32), 0.0), axis=1, keepdims=True
            )
            - jnp.where(padding, 1.0, 0.0)
            for b in range(blocks)
        ],
        axis=0,
    )
    own_id = ids_ref[me]
    allowed = jnp.zeros_like(drawn)
    for q in range(records):
        inside = (drawn >= q * segment) & (drawn < (q + 1) * segment)
        allowed += jnp.where(inside, jnp.where(ids_ref[q] != own_id, 1.0, 0.0).astype(F32), 0.0)
    grid = (blocks * span, segment)
    reverse = (2 * here) // stages
    row_block = lax.broadcasted_iota(jnp.int32, grid, 0) // span
    frame = lax.broadcasted_iota(jnp.int32, grid, 1)
    frame_block = (frame + reverse * (segment - 1 - 2 * frame)) // block_size
    mask = jnp.where(row_block == frame_block, allowed, 0.0)
    lane = lax.broadcasted_iota(jnp.int32, (blocks * span, 2 * segment), 1).astype(F32)

    def gathered(c):
        units = pool[pl.ds(c * 2, 2)].reshape(2 * segment, depth)
        first_row = (c * (2 * segment)).astype(F32)
        chosen = jnp.where(drawn - first_row == lane, 1.0, 0.0).astype(BF16)
        return jnp.dot(chosen, units, preferred_element_type=F32)

    loaded(7, pool.at[me])
    own_row = lax.broadcasted_iota(jnp.int32, (segment, segment), 0)
    own_column = lax.broadcasted_iota(jnp.int32, (segment, segment), 1)
    arranged = own_column == own_row + reverse * (segment - 1 - 2 * own_row)
    self_units = jnp.dot(
        jnp.where(arranged, 1.0, 0.0).astype(BF16),
        normalized(pool[me].astype(F32)),
        preferred_element_type=F32,
    ).T
    landed(pool.at[0], pass_recv_sem.at[0])
    drawn_ref[...] = gathered(chip)
    for n in range(2, 8):
        pool_arrival(n).wait_recv()
        pass_copy(n).start()
    landed(pool.at[pl.ds(0, 2)], pass_recv_sem.at[1])
    drawn_ref[...] += gathered(x_chip) + gathered(y_chip)

    landed(out_recv.at[pl.ds(0, stages - 1)], out_recv_sem.at[0])
    rows = jnp.concatenate([out_recv[s] for s in range(stages)], axis=0).astype(F32)
    radius = jnp.sqrt(jnp.sum(rows * rows, axis=0, keepdims=True) + EPSILON)
    unit_rows = rows * (1.0 / radius)
    anchors = unit_rows.astype(BF16)
    positive = jnp.exp(jnp.sum(anchors.astype(F32) * self_units, axis=0, keepdims=True) * INVERSE_TEMP)
    alignment = jnp.sum(unit_rows * self_units, axis=0, keepdims=True)

    landed(pool.at[0], pass_recv_sem.at[2])
    wide = drawn_ref[...] + gathered(d_chip)
    negatives = wide.astype(BF16)
    shrink = 1.0 / jnp.sqrt(jnp.sum(wide * wide, axis=-1, keepdims=True) + EPSILON)
    cosines = shrink * jnp.dot(negatives, anchors, preferred_element_type=F32)
    weights = mask * jnp.exp(cosines * INVERSE_TEMP)
    totals = positive + jnp.sum(weights, axis=0, keepdims=True)
    turned = jnp.sum(weights * cosines, axis=0, keepdims=True)
    numerator = jnp.dot((weights * shrink).T.astype(BF16), negatives, preferred_element_type=F32)
    scale = INVERSE_TEMP * LOSS_SCALE / radius
    pull = (positive / totals - 1.0) * scale
    push = scale / totals
    tilt = pull * alignment + push * turned
    chunks, _, size, _ = back_recv.shape
    for j in range(chunks):
        for s in range(stages):
            at = slice(s * channels + j * size, s * channels + (j + 1) * size)
            back_send[j, s] = (
                pull * self_units[at] + push * numerator[:, at].T - tilt * unit_rows[at]
            ).astype(BF16)
        if j:

            @pl.when(core == 1)
            def _():
                sent(back_send.at[j - 1, pl.ds(0, stages - 1)], send_sem.at[2 + j])

        for i in range(stages - 1):
            back_copy(j, far_peer(i)).start()
        back_recv[j, here] = back_send[j, here]

    half = size // 2
    shard = half // chips

    def pair_copy(which, j, lane):
        return remote(
            pair_send.at[which, j, lane], pair_recv.at[which, j],
            send_sem.at[3 + chunks], pair_recv_sem.at[which, j], (partner, here),
        )

    def spread(which, j, update):
        update = turned_over(update)
        for i in (0, 1):
            pair_send[which, j, i] = update[i * half : (i + 1) * half, :]
        pair_copy(which, j, 1 - core).start()

    def ring_copy(which, j, n):
        return remote(
            ring_send.at[which, j, near[n]], ring_recv.at[which, j, n],
            send_sem.at[4 + chunks], ring_recv_sem.at[which, j], (near[n] * 2 + core, here),
        )

    def gather(which, j):
        landed(pair_recv.at[which, j], pair_recv_sem.at[which, j])
        joined = pair_send[which, j, core].astype(F32) + pair_recv[which, j].astype(F32)
        for c in range(chips):
            ring_send[which, j, c] = joined[c * shard : (c + 1) * shard, :].astype(BF16)
        for n in (2, 0, 1):
            ring_copy(which, j, n).start()

    targets_out = (early_out, late_out)

    def share_copy(which, j, n):
        block = targets_out[which].at[j, core, chip]
        return remote(
            block, block, send_sem.at[5 + chunks], share_recv_sem.at[which, j],
            (near[n] * 2 + core, here),
        )

    def last_copy(which, j, owner):
        block = targets_out[which].at[j, core, owner]
        return remote(
            block, block, send_sem.at[6 + chunks], last_recv_sem.at[0], (partner, here)
        )

    def share(which, j):
        landed(ring_recv.at[which, j], ring_recv_sem.at[which, j])
        total = ring_send[which, j, chip].astype(F32)
        for n in range(3):
            total += ring_recv[which, j, n].astype(F32)
        targets_out[which][j, core, chip] = total.astype(BF16)
        for n in (2, 0, 1):
            share_copy(which, j, n).start()
        last_copy(which, j, chip).start()

    def relay(which, j):
        landed(ring_recv.at[which, j], share_recv_sem.at[which, j])
        for n in range(3):
            last_copy(which, j, near[n]).start()

    def backward(j):
        landed(back_recv.at[j, pl.ds(0, stages - 1)], back_recv_sem.at[j])
        lines = slice(j * size, (j + 1) * size)
        cotangent = jnp.concatenate([back_recv[j, s] for s in order], axis=1).astype(F32)
        late_drive = cotangent * second_ref[lines].astype(F32)
        update, adjoint = correlated(forward(late_drive), (hidden_spec, late_spec), lines)
        spread(1, j, update)
        hidden_grad = adjoint + late_skip[lines] * late_drive
        early_drive = hidden_grad * first_ref[lines].astype(F32)
        update, adjoint = correlated(forward(early_drive), (signal_spec, early_spec), lines)
        spread(0, j, update)
        for which in (1, 0):
            gather(which, j)
        values_out[0, lines] = turned_over(adjoint + early_skip[lines] * early_drive)
        second_out[0, lines] = turned_over(cotangent * mixed_two[lines])
        first_out[0, lines] = turned_over(hidden_grad * mixed_one[lines])

    for j in range(chunks):
        backward(j)
    for j in range(chunks):
        for which in (1, 0):
            share(which, j)
    for j in range(chunks):
        for which in (1, 0):
            relay(which, j)

    sent(pool.at[pl.ds(0, 3)], send_sem.at[0])
    sent(pool.at[pl.ds(0, 4)], send_sem.at[1])
    sent(out_send.at[pl.ds(0, stages - 1)], send_sem.at[2])
    for j in range(1, chunks):

        @pl.when(core == 0)
        def _():
            sent(back_send.at[j - 1, pl.ds(0, stages - 1)], send_sem.at[2 + j])

    sent(back_send.at[chunks - 1, pl.ds(0, stages - 1)], send_sem.at[2 + chunks])
    sent(pair_recv, send_sem.at[3 + chunks])
    sent(ring_recv, send_sem.at[4 + chunks])
    sent(ring_recv, send_sem.at[5 + chunks])
    sent(pair_recv, send_sem.at[6 + chunks])
    landed(pair_recv, last_recv_sem.at[0])


def finish(
    frames, values_in, first_in, second_in, early_in, late_in,
    values_out, first_out, second_out, early_out, late_out, early_wide, late_wide, sems,
):
    copies = [
        pltpu.make_async_copy(source, target, sems.at[i])
        for i, (source, target) in enumerate((
            (values_in, values_out), (first_in, first_out), (second_in, second_out),
            (early_wide, early_out), (late_wide, late_out),
        ))
    ]
    for copy in copies[:3]:
        copy.start()
    late_wide[...] = late_in[...].astype(F32) / frames
    copies[4].start()
    early_wide[...] = early_in[...].astype(F32) / frames
    copies[3].start()
    for copy in copies:
        copy.wait()


def local(
    records, stages,
    values, gates_first, gates_second, filter_early, filter_late, skip_early, skip_late,
    targets, negative_rows, recording_ids,
):
    _, channels, frames = values.shape
    _, segment, depth = targets.shape
    if 8 * frames * frames > TABLE_BYTES or records != 2 * GRID_CHIPS or stages % 2:
        return local_large(
            values, gates_first, gates_second, filter_early, filter_late, skip_early, skip_late,
            targets, negative_rows, recording_ids,
        )
    waves, inverse_waves, turn = tables(frames)
    chips = records // 2
    size = channels // CHUNKS
    half = size // 2
    shard = half // chips
    blocks, draws = negative_rows.shape[1:]
    vmem = pl.BlockSpec(memory_space=pltpu.VMEM)
    hbm = pl.BlockSpec(memory_space=pltpu.HBM)
    stream = pltpu.VMEM(values.shape, BF16)
    gradient = (CHUNKS, 2, chips, shard, frames)
    update = pltpu.VMEM(gradient, BF16)
    exchange = pltpu.VMEM((stages, channels, segment), BF16)
    plane = pltpu.VMEM((channels, frames), F32)
    spec = pltpu.VMEM((2, channels, frames), F32)
    back = pltpu.VMEM((CHUNKS, stages, size, segment), BF16)
    semaphores = pltpu.SemaphoreType.DMA
    results = pl.pallas_call(
        functools.partial(kernel, (records, stages)),
        out_shape=(stream, stream, stream, update, update),
        in_specs=[hbm] * 13,
        out_specs=(vmem,) * 5,
        scratch_shapes=[
            pltpu.VMEM((3, channels, frames), BF16), pltpu.VMEM((2, channels, frames), F32),
            pltpu.VMEM((2, 1, channels), F32), pltpu.VMEM((blocks, draws), jnp.int32),
            pltpu.SMEM((records,), jnp.int32), pltpu.VMEM(waves.shape, BF16),
            pltpu.VMEM(inverse_waves.shape, BF16),
            pltpu.VMEM(turn.shape, F32),
            pltpu.VMEM((records, segment, depth), BF16),
            exchange, exchange, back, back,
            pltpu.VMEM((2, CHUNKS, 2, half, frames), BF16), pltpu.VMEM((2, CHUNKS, half, frames), BF16),
            pltpu.VMEM((2, CHUNKS, chips, shard, frames), BF16),
            pltpu.VMEM((2, CHUNKS, 3, shard, frames), BF16),
            plane, plane, spec, spec, spec, spec,
            pltpu.VMEM((blocks * -(-draws // 128) * 128, depth), F32),
            semaphores((9,)), semaphores((7 + CHUNKS,)), semaphores((8,)), semaphores((3,)),
            semaphores((1,)), semaphores((CHUNKS,)), semaphores((2, CHUNKS)),
            semaphores((2, CHUNKS)), semaphores((2, CHUNKS)), semaphores((1,)),
        ],
        compiler_params=pltpu.CompilerParams(
            collective_id=0, has_side_effects=True, vmem_limit_bytes=VMEM_BYTES
        ),
    )(*(
        pltpu.with_memory_space_constraint(operand, pltpu.HBM)
        for operand in (
            values, gates_first, gates_second, filter_early, filter_late,
            skip_early[None], skip_late[None], targets, negative_rows, recording_ids,
            jnp.asarray(waves), jnp.asarray(inverse_waves), jnp.asarray(turn),
        )
    ))
    wide = gradient
    *streams, early, late = pl.pallas_call(
        functools.partial(finish, frames),
        out_shape=(jax.ShapeDtypeStruct(values.shape, BF16),) * 3 + (jax.ShapeDtypeStruct(wide, F32),) * 2,
        in_specs=[vmem] * 5,
        out_specs=(hbm,) * 5,
        scratch_shapes=[pltpu.VMEM(wide, F32), pltpu.VMEM(wide, F32), semaphores((5,))],
        compiler_params=pltpu.CompilerParams(vmem_limit_bytes=VMEM_BYTES),
    )(*results)
    return (*streams, early.reshape(channels, frames), late.reshape(channels, frames))


def solution(mesh):
    placed = (
        P("dp", "seq", None),
        P("dp", "seq", None),
        P("dp", "seq", None),
        P("seq", None),
        P("seq", None),
        P("seq"),
        P("seq"),
        P("dp", "seq", None),
        P("dp", "seq", None),
        P(),
    )
    return jax.shard_map(
        functools.partial(local, mesh.shape["dp"], mesh.shape["seq"]),
        mesh=mesh,
        in_specs=placed,
        out_specs=(
            P("dp", "seq", None),
            P("dp", "seq", None),
            P("dp", "seq", None),
            P("seq", None),
            P("seq", None),
        ),
        check_vma=False,
    )
```

```python
import functools
import math

import jax
import jax.numpy as jnp
import numpy as np
from jax import lax
from jax.experimental import pallas as pl
from jax.experimental.pallas import tpu as pltpu
from jax.sharding import PartitionSpec as P

EPSILON = 1e-06
INVERSE_TEMP = 10.0
LOSS_SCALE = 256.0
MESH = pl.DeviceIdType.MESH
F32 = jnp.float32
BF16 = jnp.bfloat16
TABLE_BYTES = 16 * 1024 * 1024
INNER_WIDTH = 128
GRID_CHIPS = 4
FINE_FILTERS = True
FINE_VALUES = True
FINE_HIDDEN = False
CHUNKS = 2
VMEM_BYTES = 40 * 1024 * 1024
HIGHEST = lax.Precision.HIGHEST


def shortened(value):

    def short(part):
        return part.astype(jnp.bfloat16) if part.dtype == jnp.float32 else part

    return jax.tree.map(short, value)


def twiddle(row_count, column_count, length, direction):
    product = (
        jnp.arange(row_count, dtype=jnp.int32)[:, None]
        * jnp.arange(column_count, dtype=jnp.int32)[None, :]
        % length
    )
    angles = direction * 2.0 * math.pi / length * product.astype(jnp.float32)
    return (jnp.cos(angles), jnp.sin(angles))


def complex_table(cosines, sines, with_imaginary):
    upper = jnp.concatenate([cosines, sines], axis=1)
    if not with_imaginary:
        return upper
    lower = jnp.concatenate([-sines, cosines], axis=1)
    return jnp.concatenate([upper, lower], axis=0)


def transform(real_part, imaginary, direction, length):
    used = real_part.shape[-1]
    with_imaginary = imaginary is not None
    outer_size = length // INNER_WIDTH
    used_rows = used // INNER_WIDTH
    lead = real_part.shape[:-1]
    folded_real = real_part.reshape(lead + (used_rows, INNER_WIDTH))
    cosines, sines = twiddle(used_rows, outer_size, outer_size, direction)
    table = complex_table(cosines, sines, with_imaginary)
    if with_imaginary:
        stacked = jnp.concatenate(
            [folded_real, imaginary.reshape(lead + (used_rows, INNER_WIDTH))], axis=-2
        )
    else:
        stacked = folded_real
    section = jnp.einsum("...ab,ak->...kb", stacked, table, precision=HIGHEST)
    section_real = section[..., :outer_size, :]
    section_imaginary = section[..., outer_size:, :]
    turn_cosine, turn_sine = twiddle(outer_size, INNER_WIDTH, length, direction)
    turned_real = section_real * turn_cosine - section_imaginary * turn_sine
    turned_imaginary = section_real * turn_sine + section_imaginary * turn_cosine
    inner_cosine, inner_sine = twiddle(INNER_WIDTH, INNER_WIDTH, INNER_WIDTH, direction)
    inner_table = complex_table(inner_cosine, inner_sine, True)
    second = jnp.einsum(
        "...ab,bk->...ak",
        jnp.concatenate([turned_real, turned_imaginary], axis=-1),
        inner_table,
        precision=HIGHEST,
    )
    final_real = jnp.swapaxes(second[..., :INNER_WIDTH], -1, -2).reshape(lead + (length,))
    final_imaginary = jnp.swapaxes(second[..., INNER_WIDTH:], -1, -2).reshape(lead + (length,))
    return (final_real, final_imaginary)


def spectrum(signal):
    return transform(signal, None, -1.0, 2 * signal.shape[-1])


def split_pair(first_signal, second_signal):
    spec_real, spec_imaginary = transform(
        first_signal, second_signal, -1.0, 2 * first_signal.shape[-1]
    )
    mirror_real = jnp.roll(jnp.flip(spec_real, -1), 1, -1)
    mirror_imaginary = jnp.roll(jnp.flip(spec_imaginary, -1), 1, -1)
    first_spec = ((spec_real + mirror_real) * 0.5, (spec_imaginary - mirror_imaginary) * 0.5)
    second_spec = ((spec_imaginary + mirror_imaginary) * 0.5, (mirror_real - spec_real) * 0.5)
    return (first_spec, second_spec)


def multiply(left_side, right_side):
    return (
        left_side[0] * right_side[0] - left_side[1] * right_side[1],
        left_side[0] * right_side[1] + left_side[1] * right_side[0],
    )


def conjugate(spec):
    return (spec[0], -spec[1])


def combine(left_side, right_side):
    return (left_side[0] - right_side[1], left_side[1] + right_side[0])


def inverse(spec, frames):
    length = spec[0].shape[-1]
    out_real, out_imaginary = transform(spec[0], spec[1], 1.0, length)
    factor = 1.0 / length
    return (out_real[..., :frames] * factor, out_imaginary[..., :frames] * factor)


def local_large(
    values,
    gates_first,
    gates_second,
    filter_early,
    filter_late,
    skip_early,
    skip_late,
    targets,
    negative_rows,
    recording_ids,
):
    signal = values[0].astype(jnp.float32)
    inner_gate = gates_first[0].astype(jnp.float32)
    outer_gate = gates_second[0].astype(jnp.float32)
    frames = signal.shape[-1]
    early_skip = skip_early[:, None]
    late_skip = skip_late[:, None]
    target_full = targets[0].astype(jnp.float32)
    unit_target = (
        target_full / jnp.sqrt(jnp.sum(target_full * target_full, axis=-1, keepdims=True) + EPSILON)
    ).astype(jnp.bfloat16)
    signal_spec, early_spec = split_pair(signal, filter_early)
    mixed_one = inverse(multiply(signal_spec, early_spec), frames)[0] + early_skip * signal
    hidden = inner_gate * mixed_one
    hidden_spec, late_spec = split_pair(hidden, filter_late)
    mixed_two = inverse(multiply(hidden_spec, late_spec), frames)[0] + late_skip * hidden
    output = outer_gate * mixed_two
    arrived = lax.all_to_all(
        output[None].astype(jnp.bfloat16), "seq", split_axis=2, concat_axis=1, tiled=True
    ).astype(jnp.float32)
    output_rows = jnp.transpose(arrived[0])
    radius = jnp.sqrt(jnp.sum(output_rows * output_rows, axis=-1, keepdims=True) + EPSILON)
    unit_rows = output_rows / radius
    anchors = unit_rows.astype(jnp.bfloat16)
    own_record = lax.axis_index("dp")
    record_count = recording_ids.shape[0]
    record_range = jnp.arange(record_count, dtype=jnp.int32)
    self_label = jnp.sum(jnp.where(record_range == own_record, recording_ids, 0))
    segment = anchors.shape[0]
    block_rows = negative_rows[0]
    block_count = block_rows.shape[0]
    block_size = segment // block_count
    column_ids = jnp.arange(segment, dtype=jnp.int32)
    initial = (
        jnp.zeros((segment,), jnp.float32),
        jnp.zeros((segment, anchors.shape[1]), jnp.float32),
    )
    shard_rows = lax.all_gather(unit_target[None], "dp", axis=0, tiled=True)

    def one_record(partial_value, member):
        pool_rows, record = member
        label = jnp.sum(jnp.where(record_range == record, recording_ids, 0))
        allowed = (label != self_label).astype(jnp.float32)
        matches = (block_rows[:, :, None] == (record * segment + column_ids)[None, None, :]).astype(
            jnp.float32
        )
        counts = jnp.sum(matches, axis=1) * allowed
        counts = jnp.broadcast_to(counts[:, None, :], (block_count, block_size, segment)).reshape(
            segment, segment
        )
        scores = (
            lax.dot_general(
                anchors, pool_rows, (((1,), (1,)), ((), ())), preferred_element_type=jnp.float32
            )
            * INVERSE_TEMP
        )
        weights = counts * jnp.exp(scores)
        numerator = jnp.dot(
            weights.astype(jnp.bfloat16), pool_rows, preferred_element_type=jnp.float32
        )
        return ((partial_value[0] + jnp.sum(weights, axis=-1), partial_value[1] + numerator), None)

    records = jnp.arange(shard_rows.shape[0], dtype=jnp.int32)
    summed = lax.scan(one_record, initial, (shard_rows, records))[0]
    unit_self = unit_target.astype(jnp.float32)
    positive = jnp.exp(jnp.sum(anchors.astype(jnp.float32) * unit_self, axis=-1) * INVERSE_TEMP)
    totals = positive + summed[0]
    anchor_grad = ((positive / totals - 1.0)[:, None] * unit_self + summed[1] / totals[:, None]) * (
        INVERSE_TEMP * LOSS_SCALE
    )
    frame_grad = (
        anchor_grad - unit_rows * jnp.sum(unit_rows * anchor_grad, axis=-1, keepdims=True)
    ) / radius
    arrived_back = lax.all_to_all(
        shortened(jnp.transpose(frame_grad)[None]), "seq", split_axis=1, concat_axis=2, tiled=True
    )
    cotangent = arrived_back[0]
    second_grad = (cotangent * mixed_two).astype(jnp.bfloat16)
    late_drive = cotangent * outer_gate
    back_late = spectrum(late_drive)
    late_pair = combine(
        multiply(back_late, conjugate(late_spec)), multiply(back_late, conjugate(hidden_spec))
    )
    hidden_back, late_update = inverse(late_pair, frames)
    hidden_grad = hidden_back + late_skip * late_drive
    first_grad = (hidden_grad * mixed_one).astype(jnp.bfloat16)
    early_drive = hidden_grad * inner_gate
    back_early = spectrum(early_drive)
    early_pair = combine(
        multiply(back_early, conjugate(early_spec)), multiply(back_early, conjugate(signal_spec))
    )
    signal_back, early_update = inverse(early_pair, frames)
    values_grad = (signal_back + early_skip * early_drive).astype(jnp.bfloat16)
    filter_sums = (
        lax.psum(early_update.astype(jnp.bfloat16), "dp").astype(jnp.float32),
        lax.psum(late_update.astype(jnp.bfloat16), "dp").astype(jnp.float32),
    )
    return (
        values_grad[None],
        first_grad[None],
        second_grad[None],
        filter_sums[0] / frames,
        filter_sums[1] / frames,
    )


def tables(frames):
    middle = frames // 2
    order = np.concatenate([np.arange(0, frames, 2), np.arange(1, frames, 2)])
    odd = 2 * order.astype(np.int64) + 1
    product = odd[None, :] * (2 * np.arange(middle, dtype=np.int64) + 1)[:, None]
    angle = np.pi / (4.0 * frames) * (product % (8 * frames))
    plus, minus = np.cos(angle) + np.sin(angle), np.cos(angle) - np.sin(angle)
    even = np.arange(frames) < middle
    ahead = np.stack([np.where(even, plus, minus), np.where(even, minus, plus)]).astype(np.float32)
    half = np.pi * odd / (4.0 * frames)
    both = np.stack([np.cos(half) + np.sin(half), np.cos(half) - np.sin(half)]) / (4.0 * frames)
    turn = np.where(even, both, both[::-1]).astype(np.float32)
    high = ahead.astype(BF16)
    low = (ahead - high.astype(np.float32)).astype(BF16)
    return np.concatenate([high, low]), np.swapaxes(high, 1, 2), turn


def kernel(
    sizes,
    values_hbm, first_hbm, second_hbm, early_hbm, late_hbm, early_skip_hbm, late_skip_hbm,
    targets_hbm, rows_hbm, ids_hbm, waves_hbm, inverse_hbm, turn_hbm,
    values_out, first_out, second_out, early_out, late_out,
    streams_ref, filters_ref, skips_ref, rows_ref, ids_ref, waves_ref, inverse_ref, turn_ref,
    pool, out_send, out_recv, back_send, back_recv, pair_send, pair_recv, ring_send, ring_recv,
    mixed_one, mixed_two, early_spec, late_spec, signal_spec, hidden_spec, drawn_ref,
    load_sem, send_sem, pool_recv_sem, pass_recv_sem, out_recv_sem, back_recv_sem,
    pair_recv_sem, ring_recv_sem, share_recv_sem, last_recv_sem,
):
    records, stages = sizes
    chips = records // 2
    me = lax.axis_index("dp")
    here = lax.axis_index("seq")
    chip, core = me // 2, me % 2
    across, along = chip % 2, chip // 2
    partner = chip * 2 + (1 - core)
    x_chip = along * 2 + (1 - across)
    y_chip = (1 - along) * 2 + across
    d_chip = (1 - along) * 2 + (1 - across)
    near = (x_chip, y_chip, d_chip)
    channels, frames = mixed_one.shape
    segment = pool.shape[1]
    depth = pool.shape[2]
    part = segment // 2

    barrier = pltpu.get_barrier_semaphore()
    peers = [(me, lax.rem(here + k, stages)) for k in range(1, stages)]
    peers += [(c * 2 + core, here) for c in near] + [(partner, here)]
    for peer in peers:
        pl.semaphore_signal(barrier, inc=1, device_id=peer, device_id_type=MESH)

    loads = [
        pltpu.make_async_copy(source, target, load_sem.at[i])
        for i, source, target in (
            (0, early_hbm, filters_ref.at[0]),
            (1, waves_hbm, waves_ref),
            (0, late_hbm, filters_ref.at[1]),
            (2, turn_hbm, turn_ref),
            (3, values_hbm.at[0], streams_ref.at[0]),
            (3, first_hbm.at[0], streams_ref.at[1]),
            (3, second_hbm.at[0], streams_ref.at[2]),
            (4, early_skip_hbm, skips_ref.at[0]),
            (4, late_skip_hbm, skips_ref.at[1]),
            (5, rows_hbm.at[0], rows_ref),
            (6, ids_hbm, ids_ref),
            (7, targets_hbm.at[0], pool.at[me]),
            (8, inverse_hbm, inverse_ref),
        )
    ]
    for load in loads:
        load.start()

    def loaded(i, ref):
        pltpu.make_async_copy(ref, ref, load_sem.at[i]).wait()

    def remote(source, target, send, recv, device):
        return pltpu.make_async_remote_copy(
            src_ref=source, dst_ref=target, send_sem=send, recv_sem=recv,
            device_id=device, device_id_type=MESH,
        )

    pl.semaphore_wait(barrier, len(peers))

    def sent(ref, sem):
        remote(ref, ref, sem, sem, (partner, here)).wait_send()

    def landed(ref, sem):
        remote(ref, ref, sem, sem, (partner, here)).wait_recv()

    def piece(owner, start, count):
        return pool.at[owner * 2 + core, pl.ds(start, count)]

    quarter = part // 2
    whole = ((part, part), (0, part), (0, part), (part, part))
    quarters = ((0, quarter), (part, quarter), (quarter, quarter), (part + quarter, quarter))
    spans = whole + quarters
    lanes = (x_chip, y_chip, x_chip, y_chip) * 2
    origins = (chip,) * 4 + (y_chip, x_chip) * 2
    arrivals = (x_chip, y_chip, x_chip, y_chip) + (d_chip,) * 4

    def pool_copy(n):
        block = piece(origins[n], *spans[n])
        source = targets_hbm.at[0, pl.ds(*spans[n])] if n < 4 else block
        return remote(
            source, block, send_sem.at[0], pool_recv_sem.at[n], (lanes[n] * 2 + core, here)
        )

    def pool_arrival(n):
        block = piece(arrivals[n], *spans[n])
        return remote(
            block, block, send_sem.at[0], pool_recv_sem.at[n], (lanes[n] * 2 + core, here)
        )

    def pass_copy(n):
        block = piece(arrivals[n], *spans[n])
        return remote(
            block, block, send_sem.at[1], pass_recv_sem.at[1 + n // 4], (partner, here)
        )

    for n in range(4):
        pool_copy(n).start()

    def normalized(rows):
        norm = jnp.sqrt(jnp.sum(rows * rows, axis=-1, keepdims=True) + EPSILON)
        return (rows * (1.0 / norm)).astype(BF16)

    middle = frames // 2
    flip_row = lax.broadcasted_iota(jnp.int32, (middle, middle), 0)
    flip_column = lax.broadcasted_iota(jnp.int32, (middle, middle), 1)
    mirror = jnp.where(flip_row + flip_column == middle - 1, 1.0, 0.0).astype(BF16)

    def halves(value):
        high = value.astype(BF16)
        return high, (value - high.astype(F32)).astype(BF16)

    def turned_over_wide(signal):
        tail = sum(
            jnp.dot(part, mirror, preferred_element_type=F32)
            for part in halves(signal[:, middle:])
        )
        return jnp.concatenate([signal[:, :middle], tail], axis=1)

    def turned_over(signal):
        signal = signal.astype(BF16)
        tail = jnp.dot(signal[:, middle:], mirror, preferred_element_type=F32).astype(BF16)
        return jnp.concatenate([signal[:, :middle], tail], axis=1)

    def forward(signal, fine=False):
        head, tail = signal[:, :middle].astype(F32), signal[:, middle:].astype(F32)
        spec = []
        for i, fold in enumerate((head + tail, head - tail)):
            high, low = halves(fold)
            wave = jnp.dot(high, waves_ref[i], preferred_element_type=F32)
            if fine:
                wave += jnp.dot(high, waves_ref[2 + i], preferred_element_type=F32)
                wave += jnp.dot(low, waves_ref[i], preferred_element_type=F32)
            spec.append(wave)
        return tuple(spec)

    def inverse(*spec):
        plus, minus = (
            jnp.dot(wave.astype(BF16), inverse_ref[i], preferred_element_type=F32)
            for i, wave in enumerate(spec)
        )
        return jnp.concatenate([plus + minus, plus - minus], axis=1)

    def unshifted(spec):
        first, second = spec
        turn_first = turn_ref[0:1, :]
        turn_second = turn_ref[1:2, :]
        return (
            first * turn_first + second * turn_second,
            first * turn_second - second * turn_first,
        )

    def keep(ref, spec):
        ref[0] = spec[0]
        ref[1] = spec[1]

    def convolved(spec, ref):
        first, second = spec
        return inverse(first * ref[0] + second * ref[1], second * ref[0] - first * ref[1])

    def correlated(spec, refs, lines):
        first, second = spec
        waves = []
        for ref in refs:
            real, imaginary = ref[0, lines], ref[1, lines]
            waves.append((first * real - second * imaginary, second * real + first * imaginary))
        joined = inverse(*(jnp.concatenate(wave, axis=0) for wave in zip(*waves)))
        count = joined.shape[0] // len(refs)
        return [joined[i * count : (i + 1) * count] for i in range(len(refs))]

    def column(row):
        return jnp.broadcast_to(row, (8, channels)).T[:, 0:1]

    loaded(0, filters_ref)
    loaded(1, waves_ref)
    loaded(2, turn_ref)
    keep(early_spec, unshifted(forward(turned_over_wide(filters_ref[0]), FINE_FILTERS)))
    keep(late_spec, unshifted(forward(turned_over_wide(filters_ref[1]), FINE_FILTERS)))
    loaded(3, streams_ref)
    loaded(4, skips_ref)
    values_ref, first_ref, second_ref = (streams_ref.at[i] for i in range(3))
    for ref in (values_ref, first_ref, second_ref):
        ref[...] = turned_over(ref[...])
    loaded(8, inverse_ref)
    early_skip = column(skips_ref[0])
    late_skip = column(skips_ref[1])
    spec = forward(values_ref[...], FINE_VALUES)
    mixed_one[...] = convolved(spec, early_spec) + early_skip * values_ref[...].astype(F32)
    signal_waves = spec
    hidden = first_ref[...].astype(F32) * mixed_one[...]
    spec = forward(hidden, FINE_HIDDEN)
    mixed_two[...] = convolved(spec, late_spec) + late_skip * hidden

    output = second_ref[...].astype(F32) * mixed_two[...]
    order = [s if 2 * s < stages else stages - 1 - s + stages // 2 for s in range(stages)]
    for i, s in enumerate(order):
        out_send[s] = output[:, i * segment : (i + 1) * segment].astype(BF16)

    low_side = 1 - (2 * here) // stages

    def far_peer(j):
        high = stages - 1 - j
        up = high - (here - high + stages) // stages
        down = j + (j - here + stages) // stages
        return low_side * up + (1 - low_side) * down

    def out_copy(peer):
        return remote(
            out_send.at[peer], out_recv.at[here], send_sem.at[2], out_recv_sem.at[0], (me, peer)
        )

    def back_copy(j, peer):
        return remote(
            back_send.at[j, peer], back_recv.at[j, here],
            send_sem.at[3 + j], back_recv_sem.at[j], (me, peer),
        )

    for j in range(stages - 1):
        out_copy(far_peer(j)).start()
    out_recv[here] = out_send[here]

    remote(
        targets_hbm.at[0], pool.at[me], send_sem.at[1], pass_recv_sem.at[0], (partner, here)
    ).start()
    pool_arrival(1).wait_recv()
    pool_copy(4).start()
    pool_copy(6).start()
    pass_copy(1).start()
    pool_arrival(0).wait_recv()
    pool_copy(5).start()
    pool_copy(7).start()
    pass_copy(0).start()

    keep(signal_spec, unshifted(signal_waves))
    keep(hidden_spec, unshifted(spec))

    loaded(5, rows_ref)
    loaded(6, ids_ref)
    blocks, draws = rows_ref.shape
    block_size = segment // blocks
    span = drawn_ref.shape[0] // blocks
    place = lax.broadcasted_iota(jnp.int32, (span, draws), 0)
    diagonal = place == lax.broadcasted_iota(jnp.int32, (span, draws), 1)
    padding = lax.broadcasted_iota(jnp.int32, (span, 1), 0) >= draws
    drawn = jnp.concatenate(
        [
            jnp.sum(
                jnp.where(diagonal, rows_ref[b : b + 1, :].astype(F32), 0.0), axis=1, keepdims=True
            )
            - jnp.where(padding, 1.0, 0.0)
            for b in range(blocks)
        ],
        axis=0,
    )
    own_id = ids_ref[me]
    allowed = jnp.zeros_like(drawn)
    for q in range(records):
        inside = (drawn >= q * segment) & (drawn < (q + 1) * segment)
        allowed += jnp.where(inside, jnp.where(ids_ref[q] != own_id, 1.0, 0.0).astype(F32), 0.0)
    grid = (blocks * span, segment)
    reverse = (2 * here) // stages
    row_block = lax.broadcasted_iota(jnp.int32, grid, 0) // span
    frame = lax.broadcasted_iota(jnp.int32, grid, 1)
    frame_block = (frame + reverse * (segment - 1 - 2 * frame)) // block_size
    mask = jnp.where(row_block == frame_block, allowed, 0.0)
    lane = lax.broadcasted_iota(jnp.int32, (blocks * span, 2 * segment), 1).astype(F32)

    def gathered(c):
        units = pool[pl.ds(c * 2, 2)].reshape(2 * segment, depth)
        first_row = (c * (2 * segment)).astype(F32)
        chosen = jnp.where(drawn - first_row == lane, 1.0, 0.0).astype(BF16)
        return jnp.dot(chosen, units, preferred_element_type=F32)

    loaded(7, pool.at[me])
    own_row = lax.broadcasted_iota(jnp.int32, (segment, segment), 0)
    own_column = lax.broadcasted_iota(jnp.int32, (segment, segment), 1)
    arranged = own_column == own_row + reverse * (segment - 1 - 2 * own_row)
    self_units = jnp.dot(
        jnp.where(arranged, 1.0, 0.0).astype(BF16),
        normalized(pool[me].astype(F32)),
        preferred_element_type=F32,
    ).T
    landed(pool.at[0], pass_recv_sem.at[0])
    drawn_ref[...] = gathered(chip)
    for n in range(2, 8):
        pool_arrival(n).wait_recv()
        pass_copy(n).start()
    landed(pool.at[pl.ds(0, 2)], pass_recv_sem.at[1])
    drawn_ref[...] += gathered(x_chip) + gathered(y_chip)

    landed(out_recv.at[pl.ds(0, stages - 1)], out_recv_sem.at[0])
    rows = jnp.concatenate([out_recv[s] for s in range(stages)], axis=0).astype(F32)
    radius = jnp.sqrt(jnp.sum(rows * rows, axis=0, keepdims=True) + EPSILON)
    unit_rows = rows * (1.0 / radius)
    anchors = unit_rows.astype(BF16)
    positive = jnp.exp(jnp.sum(anchors.astype(F32) * self_units, axis=0, keepdims=True) * INVERSE_TEMP)
    alignment = jnp.sum(unit_rows * self_units, axis=0, keepdims=True)

    landed(pool.at[0], pass_recv_sem.at[2])
    wide = drawn_ref[...] + gathered(d_chip)
    negatives = wide.astype(BF16)
    shrink = 1.0 / jnp.sqrt(jnp.sum(wide * wide, axis=-1, keepdims=True) + EPSILON)
    cosines = shrink * jnp.dot(negatives, anchors, preferred_element_type=F32)
    weights = mask * jnp.exp(cosines * INVERSE_TEMP)
    totals = positive + jnp.sum(weights, axis=0, keepdims=True)
    turned = jnp.sum(weights * cosines, axis=0, keepdims=True)
    numerator = jnp.dot((weights * shrink).T.astype(BF16), negatives, preferred_element_type=F32)
    scale = INVERSE_TEMP * LOSS_SCALE / radius
    pull = (positive / totals - 1.0) * scale
    push = scale / totals
    tilt = pull * alignment + push * turned
    chunks, _, size, _ = back_recv.shape
    for j in range(chunks):
        for s in range(stages):
            at = slice(s * channels + j * size, s * channels + (j + 1) * size)
            back_send[j, s] = (
                pull * self_units[at] + push * numerator[:, at].T - tilt * unit_rows[at]
            ).astype(BF16)
        if j:

            @pl.when(core == 1)
            def _():
                sent(back_send.at[j - 1, pl.ds(0, stages - 1)], send_sem.at[2 + j])

        for i in range(stages - 1):
            back_copy(j, far_peer(i)).start()
        back_recv[j, here] = back_send[j, here]

    half = size // 2
    shard = half // chips

    def pair_copy(which, j, lane):
        return remote(
            pair_send.at[which, j, lane], pair_recv.at[which, j],
            send_sem.at[3 + chunks], pair_recv_sem.at[which, j], (partner, here),
        )

    def spread(which, j, update):
        update = turned_over(update)
        for i in (0, 1):
            pair_send[which, j, i] = update[i * half : (i + 1) * half, :]
        pair_copy(which, j, 1 - core).start()

    def ring_copy(which, j, n):
        return remote(
            ring_send.at[which, j, near[n]], ring_recv.at[which, j, n],
            send_sem.at[4 + chunks], ring_recv_sem.at[which, j], (near[n] * 2 + core, here),
        )

    def gather(which, j):
        landed(pair_recv.at[which, j], pair_recv_sem.at[which, j])
        joined = pair_send[which, j, core].astype(F32) + pair_recv[which, j].astype(F32)
        for c in range(chips):
            ring_send[which, j, c] = joined[c * shard : (c + 1) * shard, :].astype(BF16)
        for n in (2, 0, 1):
            ring_copy(which, j, n).start()

    targets_out = (early_out, late_out)

    def share_copy(which, j, n):
        block = targets_out[which].at[j, core, chip]
        return remote(
            block, block, send_sem.at[5 + chunks], share_recv_sem.at[which, j],
            (near[n] * 2 + core, here),
        )

    def last_copy(which, j, owner):
        block = targets_out[which].at[j, core, owner]
        return remote(
            block, block, send_sem.at[6 + chunks], last_recv_sem.at[0], (partner, here)
        )

    def share(which, j):
        landed(ring_recv.at[which, j], ring_recv_sem.at[which, j])
        total = ring_send[which, j, chip].astype(F32)
        for n in range(3):
            total += ring_recv[which, j, n].astype(F32)
        targets_out[which][j, core, chip] = total.astype(BF16)
        for n in (2, 0, 1):
            share_copy(which, j, n).start()
        last_copy(which, j, chip).start()

    def relay(which, j):
        landed(ring_recv.at[which, j], share_recv_sem.at[which, j])
        for n in range(3):
            last_copy(which, j, near[n]).start()

    def backward(j):
        landed(back_recv.at[j, pl.ds(0, stages - 1)], back_recv_sem.at[j])
        lines = slice(j * size, (j + 1) * size)
        cotangent = jnp.concatenate([back_recv[j, s] for s in order], axis=1).astype(F32)
        late_drive = cotangent * second_ref[lines].astype(F32)
        update, adjoint = correlated(forward(late_drive), (hidden_spec, late_spec), lines)
        spread(1, j, update)
        hidden_grad = adjoint + late_skip[lines] * late_drive
        early_drive = hidden_grad * first_ref[lines].astype(F32)
        spec = forward(early_drive)
        spread(0, j, correlated(spec, (signal_spec,), lines)[0])
        for which in (1, 0):
            gather(which, j)
        def outs():
            adjoint = correlated(spec, (early_spec,), lines)[0]
            values_out[0, lines] = turned_over(adjoint + early_skip[lines] * early_drive)
            second_out[0, lines] = turned_over(cotangent * mixed_two[lines])
            first_out[0, lines] = turned_over(hidden_grad * mixed_one[lines])

        return outs

    results = [backward(j) for j in range(chunks)]
    for which in (1, 0):
        share(which, 0)
    for result in results:
        result()
    for j in range(1, chunks):
        for which in (1, 0):
            share(which, j)
    for j in range(chunks):
        for which in (1, 0):
            relay(which, j)

    sent(pool.at[pl.ds(0, 3)], send_sem.at[0])
    sent(pool.at[pl.ds(0, 4)], send_sem.at[1])
    sent(out_send.at[pl.ds(0, stages - 1)], send_sem.at[2])
    for j in range(1, chunks):

        @pl.when(core == 0)
        def _():
            sent(back_send.at[j - 1, pl.ds(0, stages - 1)], send_sem.at[2 + j])

    sent(back_send.at[chunks - 1, pl.ds(0, stages - 1)], send_sem.at[2 + chunks])
    sent(pair_recv, send_sem.at[3 + chunks])
    sent(ring_recv, send_sem.at[4 + chunks])
    sent(ring_recv, send_sem.at[5 + chunks])
    sent(pair_recv, send_sem.at[6 + chunks])
    landed(pair_recv, last_recv_sem.at[0])


def finish(
    frames, values_in, first_in, second_in, early_in, late_in,
    values_out, first_out, second_out, early_out, late_out, early_wide, late_wide, sems,
):
    copies = [
        pltpu.make_async_copy(source, target, sems.at[i])
        for i, (source, target) in enumerate((
            (values_in, values_out), (first_in, first_out), (second_in, second_out),
            (early_wide, early_out), (late_wide, late_out),
        ))
    ]
    for copy in copies[:3]:
        copy.start()
    late_wide[...] = late_in[...].astype(F32) / frames
    copies[4].start()
    early_wide[...] = early_in[...].astype(F32) / frames
    copies[3].start()
    for copy in copies:
        copy.wait()


def local(
    records, stages,
    values, gates_first, gates_second, filter_early, filter_late, skip_early, skip_late,
    targets, negative_rows, recording_ids,
):
    _, channels, frames = values.shape
    _, segment, depth = targets.shape
    if 8 * frames * frames > TABLE_BYTES or records != 2 * GRID_CHIPS or stages % 2:
        return local_large(
            values, gates_first, gates_second, filter_early, filter_late, skip_early, skip_late,
            targets, negative_rows, recording_ids,
        )
    waves, inverse_waves, turn = tables(frames)
    chips = records // 2
    size = channels // CHUNKS
    half = size // 2
    shard = half // chips
    blocks, draws = negative_rows.shape[1:]
    vmem = pl.BlockSpec(memory_space=pltpu.VMEM)
    hbm = pl.BlockSpec(memory_space=pltpu.HBM)
    stream = pltpu.VMEM(values.shape, BF16)
    gradient = (CHUNKS, 2, chips, shard, frames)
    update = pltpu.VMEM(gradient, BF16)
    exchange = pltpu.VMEM((stages, channels, segment), BF16)
    plane = pltpu.VMEM((channels, frames), F32)
    spec = pltpu.VMEM((2, channels, frames), F32)
    back = pltpu.VMEM((CHUNKS, stages, size, segment), BF16)
    semaphores = pltpu.SemaphoreType.DMA
    results = pl.pallas_call(
        functools.partial(kernel, (records, stages)),
        out_shape=(stream, stream, stream, update, update),
        in_specs=[hbm] * 13,
        out_specs=(vmem,) * 5,
        scratch_shapes=[
            pltpu.VMEM((3, channels, frames), BF16), pltpu.VMEM((2, channels, frames), F32),
            pltpu.VMEM((2, 1, channels), F32), pltpu.VMEM((blocks, draws), jnp.int32),
            pltpu.SMEM((records,), jnp.int32), pltpu.VMEM(waves.shape, BF16),
            pltpu.VMEM(inverse_waves.shape, BF16),
            pltpu.VMEM(turn.shape, F32),
            pltpu.VMEM((records, segment, depth), BF16),
            exchange, exchange, back, back,
            pltpu.VMEM((2, CHUNKS, 2, half, frames), BF16), pltpu.VMEM((2, CHUNKS, half, frames), BF16),
            pltpu.VMEM((2, CHUNKS, chips, shard, frames), BF16),
            pltpu.VMEM((2, CHUNKS, 3, shard, frames), BF16),
            plane, plane, spec, spec, spec, spec,
            pltpu.VMEM((blocks * -(-draws // 128) * 128, depth), F32),
            semaphores((9,)), semaphores((7 + CHUNKS,)), semaphores((8,)), semaphores((3,)),
            semaphores((1,)), semaphores((CHUNKS,)), semaphores((2, CHUNKS)),
            semaphores((2, CHUNKS)), semaphores((2, CHUNKS)), semaphores((1,)),
        ],
        compiler_params=pltpu.CompilerParams(
            collective_id=0, has_side_effects=True, vmem_limit_bytes=VMEM_BYTES
        ),
    )(*(
        pltpu.with_memory_space_constraint(operand, pltpu.HBM)
        for operand in (
            values, gates_first, gates_second, filter_early, filter_late,
            skip_early[None], skip_late[None], targets, negative_rows, recording_ids,
            jnp.asarray(waves), jnp.asarray(inverse_waves), jnp.asarray(turn),
        )
    ))
    wide = gradient
    *streams, early, late = pl.pallas_call(
        functools.partial(finish, frames),
        out_shape=(jax.ShapeDtypeStruct(values.shape, BF16),) * 3 + (jax.ShapeDtypeStruct(wide, F32),) * 2,
        in_specs=[vmem] * 5,
        out_specs=(hbm,) * 5,
        scratch_shapes=[pltpu.VMEM(wide, F32), pltpu.VMEM(wide, F32), semaphores((5,))],
        compiler_params=pltpu.CompilerParams(vmem_limit_bytes=VMEM_BYTES),
    )(*results)
    return (*streams, early.reshape(channels, frames), late.reshape(channels, frames))


def solution(mesh):
    placed = (
        P("dp", "seq", None),
        P("dp", "seq", None),
        P("dp", "seq", None),
        P("seq", None),
        P("seq", None),
        P("seq"),
        P("seq"),
        P("dp", "seq", None),
        P("dp", "seq", None),
        P(),
    )
    return jax.shard_map(
        functools.partial(local, mesh.shape["dp"], mesh.shape["seq"]),
        mesh=mesh,
        in_specs=placed,
        out_specs=(
            P("dp", "seq", None),
            P("dp", "seq", None),
            P("dp", "seq", None),
            P("seq", None),
            P("seq", None),
        ),
        check_vma=False,
    )
```
